256 devices in a mesh: expert: 32 (over x, z), seq: 4 (over y_lo, core), fsdp: 2 (over y_hi).
Axes of the slice: x: 4, y: 4 (y_hi: 2, y_lo: 2; y = y_hi * 2 + y_lo), z: 8, core: 2. Of those that a mesh axis runs over, the one named last changes fastest.
Arguments:
- tokens: float32 [57344, 1280], P(('expert', 'seq', 'fsdp')), may hold values from -100 to 100
- slot_params: float32 [1280, 256], replicated, may hold values from -4 to 4
- w_in: float32 [64, 2560, 1280], P('expert', ('seq', 'fsdp')), may hold values from -0.15625 to 0.15625
- w_out: float32 [64, 2560, 1280], P('expert', ('seq', 'fsdp')), may hold values from -0.125 to 0.125
Outputs:
- mixed: float32 [57344, 1280], P(('expert', 'seq', 'fsdp'))
The draws below stay inside these ranges and needn't reach their ends.
All inputs are finite; a program needn't handle non-finite values.
Results may differ from the reference program's by a relative error of at most 0.0003.
Values sent between devices are 32-bit elements; how exact they have to be, the bound alone decides.
A program may use at most 64 MiB of HBM per device.

```python
import math
import jax
import jax.numpy as jnp
from jax import lax

D = 1280
MLP = 2560
SLOTS = 4
EXPERTS = 64
TOKENS = 57344


def slot_matrix(key):
    folded = jax.random.fold_in(key, 11)
    keys = jax.random.split(folded, 2)
    columns = EXPERTS * SLOTS
    gains = jnp.exp(jax.random.uniform(keys[0], (1, columns), jnp.float32, math.log(3.0), math.log(6.0)))
    values_drawn = jnp.clip(jax.random.normal(keys[1], (D, columns), jnp.float32), -5.0, 5.0)
    return values_drawn * gains / math.sqrt(D)


def draw_slot_params(key, part):
    return slot_matrix(key)


def draw_tokens(key, part):
    folded = jax.random.fold_in(key, 23)
    keys = jax.random.split(folded, 1)
    values_drawn = jnp.clip(jax.random.normal(keys[0], (TOKENS, D), jnp.float32), -6.0, 6.0)
    return values_drawn


def level_of(own_key, shape, shards, smallest, top_value):
    factor_of = 1.0
    for dim, blocks in shards:
        draws = jax.random.uniform(jax.random.fold_in(jax.random.fold_in(own_key, 6), dim), (blocks,), jnp.float32, smallest / len(shards), top_value / len(shards))
        factor_of = factor_of * jnp.repeat(jnp.exp(draws), shape[dim] // blocks).reshape((-1,) + (1,) * (len(shape) - 1 - dim))
    return factor_of


def gaussian(own_key, dims, scale, bound, cuts=(), kind=jnp.bfloat16):
    loudness = level_of(own_key, dims, cuts, -0.22, 0.18) if cuts else 1.0
    array = jax.random.normal(own_key, dims, jnp.float32) * scale * loudness
    return jnp.minimum(jnp.maximum(array, -bound), bound).astype(kind)


def setup_inputs(seed: int = 0) -> dict:
    splits = jax.random.split(jax.random.key(seed), 5)
    tokens = draw_tokens(jax.random.fold_in(splits[4], 71), 0)
    slot_params = draw_slot_params(jax.random.fold_in(splits[4], 71), 0)
    w_in = gaussian(splits[2], (EXPERTS, MLP, D), D ** -0.5, 0.15625, ((0, 32), (1, 8)), jnp.float32)
    w_out = gaussian(splits[3], (EXPERTS, MLP, D), MLP ** -0.5, 0.125, ((0, 32), (1, 8)), jnp.float32)
    return dict(tokens=tokens, slot_params=slot_params, w_in=w_in, w_out=w_out)


def reference(tokens, slot_params, w_in, w_out):
    highest = lax.Precision.HIGHEST
    logits = jnp.dot(tokens, slot_params, precision=highest, preferred_element_type=jnp.float32)
    slot_peak = jnp.max(logits, axis=0, keepdims=True)
    weights = jnp.exp(logits - slot_peak)
    slot_mass = jnp.sum(weights, axis=0)
    slot_sums = jnp.dot(weights.T, tokens, precision=highest, preferred_element_type=jnp.float32)
    slot_inputs = (slot_sums / slot_mass[:, None]).reshape(EXPERTS, SLOTS, D)
    hidden = jax.nn.gelu(jnp.einsum("esd,ehd->esh", slot_inputs, w_in, precision=highest), approximate=False)
    slot_outputs = jnp.einsum("esh,ehd->esd", hidden, w_out, precision=highest).reshape(EXPERTS * SLOTS, D)
    row_peak = jnp.max(logits, axis=1, keepdims=True)
    row_exp = jnp.exp(logits - row_peak)
    combine = row_exp / jnp.sum(row_exp, axis=1, keepdims=True)
    return jnp.dot(combine, slot_outputs, precision=highest, preferred_element_type=jnp.float32)
```

```python
import functools

import jax
import jax.numpy as jnp
from jax import lax
from jax.experimental import pallas as pl
from jax.experimental.pallas import tpu as pltpu
from jax.sharding import Mesh
from jax.sharding import PartitionSpec as P

AXES = ("x", "z", "y_lo", "core", "y_hi")
F32 = jnp.float32
BF16 = jnp.bfloat16
SLOTS = 4
HALF = 640
WIDE = HALF + 128


def split(a):
    hi = a.astype(BF16)
    return hi, (a - hi.astype(F32)).astype(BF16)


def dot(a, b, dims=(((1,), (0,)), ((), ()))):
    return lax.dot_general(a, b, dims, preferred_element_type=F32)


def dot3(ah, al, bh, bl, dims=(((1,), (0,)), ((), ()))):
    return dot(ah, bh, dims) + (dot(ah, bl, dims) + dot(al, bh, dims))


def peak_or_mass(peak, mass, rows):
    lane = lax.broadcasted_iota(jnp.int32, (rows, 128), 1)
    return jnp.where(lane < 64, peak, mass)


def merged(parts):
    peaks = [p[:, HALF : HALF + 1] for p in parts]
    peak = functools.reduce(jnp.maximum, peaks)
    total = None
    for part, own in zip(parts, peaks):
        scaled = part * jnp.exp(own - peak)
        total = scaled if total is None else total + scaled
    rows = total.shape[0]
    return total[:, :HALF], peak_or_mass(peak, total[:, HALF + 64 : HALF + 65], rows)


def layer_kernel(
    NX, NY, NZ, stop,
    tok_hbm, par_hbm, win_hbm, wout_hbm, out_ref,
    tok, par, win, wout, xh, xl, wih, wil, woh, wol,
    tmp, ext, wth, wtl, ch, cl, sums, recv_c, kept,
    recv_a, recv_b, two_a, two_b, recv_a2, recv_b2, zsend, zrecv, inputs, osend, orecv, zout, full,
    ld, sc, rc, s1, r1, s2, r2, s3, r3, s4, r4, s5, r5, s6, r6, s7, r7, s8, r8, s9, r9,
):
    x, z, y_lo, c, y_hi = (lax.axis_index(a) for a in AXES)
    y = y_hi * 2 + y_lo
    tokens, width = tok.shape
    K = 2 * NY
    NXZ = NX * NZ

    def device(dx=0, dy=0, dz=0, dc=0):
        to_y = lax.rem(y + dy, NY)
        return (
            lax.rem(x + dx, NX), lax.rem(z + dz, NZ), lax.rem(to_y, 2),
            lax.rem(c + dc, 2), lax.div(to_y, 2),
        )

    def remote(src, dst, send, recv, **to):
        return pltpu.make_async_remote_copy(
            src_ref=src, dst_ref=dst, send_sem=send, recv_sem=recv,
            device_id=device(**to), device_id_type=pl.DeviceIdType.MESH,
        )

    def put(a):
        for b in range(tmp.shape[0]):
            tmp[b] = a[:, 128 * b : 128 * (b + 1)]

    def every_kth(k):
        return jnp.concatenate([tmp[b, pl.ds(k, NXZ, stride=K), :] for b in range(tmp.shape[0])], axis=1)

    xs, ys, zs = (
        sorted(range(1, n), key=lambda d: -min(d, n - d)) for n in (NX, NY, NZ)
    )
    column = [(dy, dc) for dy in [*ys, 0] for dc in (1, 0) if (dy, dc) != (0, 0)]

    barrier = pltpu.get_barrier_semaphore()
    peers = [dict(dx=d) for d in xs] + [dict(dz=d) for d in zs] + [dict(dy=d, dc=e) for d, e in column]
    for to in peers:
        pl.semaphore_signal(barrier, inc=1, device_id=device(**to), device_id_type=pl.DeviceIdType.MESH)

    steps = width // 256
    loads = []
    for i in range(steps):
        at = pl.ds(256 * i, 256)
        loads.append(pltpu.make_async_copy(tok_hbm.at[:, at], tok.at[:, at], ld.at[2 * i]))
        loads.append(pltpu.make_async_copy(par_hbm.at[at, :], par.at[at, :], ld.at[2 * i + 1]))
    load_win = pltpu.make_async_copy(win_hbm, win, ld.at[2 * steps])
    load_wout = pltpu.make_async_copy(wout_hbm, wout, ld.at[2 * steps + 1])
    for copy in [*loads, load_win, load_wout]:
        copy.start()

    n_slots = par.shape[1]
    pad = xh.shape[0] - tokens
    logits = jnp.zeros((tokens, n_slots), F32)
    for i in range(steps):
        loads[2 * i].wait()
        loads[2 * i + 1].wait()
        at = slice(256 * i, 256 * (i + 1))
        a_hi, a_lo = split(tok[:, at])
        b_hi, b_lo = split(par[at, :])
        xh[0:tokens, at] = a_hi
        xl[0:tokens, at] = a_lo
        logits += dot3(a_hi, a_lo, b_hi, b_lo)
    xh[tokens:, :] = jnp.zeros((pad, width), BF16)
    xl[tokens:, :] = jnp.zeros((pad, width), BF16)

    by_slot = jnp.concatenate([logits, jnp.zeros((pad, n_slots), F32)], axis=0).T
    lane = lax.broadcasted_iota(jnp.int32, by_slot.shape, 1)
    held = lane < tokens
    by_slot = jnp.where(held, by_slot, -3e38)
    peak = jnp.max(by_slot, axis=1, keepdims=True)
    weights = jnp.where(held, jnp.exp(by_slot - peak), 0.0)
    put(weights)
    ext[...] = peak_or_mass(peak, jnp.sum(weights, axis=1, keepdims=True), n_slots)
    for k in range(K):
        row = (k % 2) * (NY * NXZ) + (k // 2) * NXZ
        hi, lo = split(every_kth(k))
        wth[row : row + NXZ, :] = hi
        wtl[row : row + NXZ, :] = lo
        block = ext[pl.ds(k, NXZ, stride=K), :].reshape(NX, NZ, 128)
        for p in range(2):
            sums[p, k % 2, k // 2, :, :, HALF:] = block

    pl.semaphore_wait(barrier, len(peers))
    sends = []
    other = 1 - c
    for p in range(2):
        at = slice(HALF * p, HALF * (p + 1))
        part = dot3(wth[...], wtl[...], xh[:, at], xl[:, at])
        sums[p, :, :, :, :, :HALF] = part.reshape(2, NY, NX, NZ, HALF)
        sends.append(remote(sums.at[p, other], recv_c.at[p], sc.at[p], rc.at[p], dc=1))
        sends[-1].start()

    def fill_weights():
        load_win.wait()
        load_wout.wait()
        wih[...], wil[...] = split(win[...])
        woh[...], wol[...] = split(wout[...])

    def fill_combine():
        row_exp = jnp.exp(logits - jnp.max(logits, axis=1, keepdims=True))
        combine = row_exp / jnp.sum(row_exp, axis=1, keepdims=True)
        put(jnp.concatenate([combine, jnp.zeros((pad, n_slots), F32)], axis=0).T)
        order = [every_kth(2 * b + a) for a in range(2) for b in range(NY)]
        ch[...], cl[...] = split(jnp.concatenate(order, axis=0).T[:tokens])

    def joined(p, yi, xi):
        return merged([sums[p, c, yi, xi], recv_c[p, yi, xi]])

    sends[0].wait_recv()
    stage1 = []
    for i, dy in enumerate([*ys, 0]):
        to = lax.rem(y + dy, NY)
        for xi in range(NX):
            kept[0, to, xi, :, :HALF], kept[0, to, xi, :, HALF:] = joined(0, to, xi)
        if dy:
            stage1.append(remote(kept.at[0, to], recv_a.at[dy - 1], s1.at[dy - 1], r1.at[dy - 1], dy=dy))
            stage1[-1].start()
    sends[1].wait_recv()
    for i, dx in enumerate([*xs, 0]):
        to = lax.rem(x + dx, NX)
        for yi in range(NY):
            kept[1, yi, to, :, :HALF], kept[1, yi, to, :, HALF:] = joined(1, yi, to)
        if dx:
            stage1.append(remote(kept.at[1, :, to], recv_b.at[dx - 1], s2.at[dx - 1], r2.at[dx - 1], dx=dx))
            stage1[-1].start()
    fill_weights()

    for copy in stage1[: len(ys)]:
        copy.wait_recv()
    stage2 = []
    for dx in [*xs, 0]:
        to = lax.rem(x + dx, NX)
        two_a[to, :, :HALF], two_a[to, :, HALF:] = merged([kept[0, y, to]] + [recv_a[d, to] for d in range(NY - 1)])
        if dx:
            stage2.append(remote(two_a.at[to], recv_a2.at[dx - 1], s3.at[dx - 1], r3.at[dx - 1], dx=dx))
            stage2[-1].start()
    for copy in stage1[len(ys) :]:
        copy.wait_recv()
    for dy in [*ys, 0]:
        to = lax.rem(y + dy, NY)
        two_b[to, :, :HALF], two_b[to, :, HALF:] = merged([kept[1, to, x]] + [recv_b[d, to] for d in range(NX - 1)])
        if dy:
            stage2.append(remote(two_b.at[to], recv_b2.at[dy - 1], s4.at[dy - 1], r4.at[dy - 1], dy=dy))
            stage2[-1].start()
    fill_combine()

    for copy in stage2:
        copy.wait_recv()
    rows_a = jnp.concatenate(merged([two_a[x]] + [recv_a2[d] for d in range(NX - 1)]), axis=1)
    rows_b = jnp.concatenate(merged([two_b[y]] + [recv_b2[d] for d in range(NY - 1)]), axis=1)
    for i in range(NZ):
        zsend[i, :, :WIDE] = rows_a[i : i + 1]
        zsend[i, :, WIDE:] = rows_b[i : i + 1]
    stage3 = []
    for dz in zs:
        to = lax.rem(z + dz, NZ)
        stage3.append(remote(zsend.at[to], zrecv.at[dz], s5.at[dz - 1], r5.at[dz - 1], dz=dz))
        stage3[-1].start()
    zrecv[0] = zsend[z]
    for copy in stage3:
        copy.wait_recv()
    k = y * 2 + c
    got = zrecv[...].reshape(NZ, 2 * WIDE)
    for p in range(2):
        part = got[:, WIDE * p : WIDE * (p + 1)]
        own = part[:, HALF : HALF + 1]
        total = jnp.sum(part * jnp.exp(own - jnp.max(own, axis=0, keepdims=True)), axis=0, keepdims=True)
        inputs[k, :, HALF * p : HALF * (p + 1)] = total[:, :HALF] / total[:, HALF + 64 : HALF + 65]

    stage4 = []
    for i, (dy, dc) in enumerate(column):
        stage4.append(remote(inputs.at[k], inputs.at[k], s6.at[i], r6.at[i], dy=dy, dc=dc))
        stage4[-1].start()
    for copy in stage4:
        copy.wait_recv()
    s_hi, s_lo = split(inputs[...].reshape(K, width))
    for e in range(K // SLOTS):
        rows = slice(SLOTS * e, SLOTS * (e + 1))
        v = dot3(s_hi[rows], s_lo[rows], wih[e], wil[e], (((1,), (1,)), ((), ())))
        hidden = v * (1.0 + lax.erf(v * 0.7071067811865476)) * 0.5
        h_hi, h_lo = split(hidden)
        partial = dot3(h_hi, h_lo, woh[e], wol[e])
        for i in range(SLOTS):
            osend[SLOTS * e + i] = partial[i : i + 1]
    stage5 = []
    for i, (dy, dc) in enumerate(column):
        to = lax.rem(y + dy, NY) * 2 + lax.rem(c + dc, 2)
        stage5.append(remote(osend.at[to], orecv.at[i], s7.at[i], r7.at[i], dy=dy, dc=dc))
        stage5[-1].start()
    for copy in stage5:
        copy.wait_recv()
    total = osend[k]
    for i in range(len(column)):
        total += orecv[i]
    zout[z] = total

    stage6 = []
    for dz in zs:
        stage6.append(remote(zout.at[z], zout.at[z], s8.at[dz - 1], r8.at[dz - 1], dz=dz))
        stage6[-1].start()
    for copy in stage6:
        copy.wait_recv()
    rows = zout[...].reshape(NZ, width)
    full[0, c, y, x] = rows[:, :HALF]
    full[1, c, y, x] = rows[:, HALF:]
    stage7 = []
    n = 0

    def spread(ref, **to):
        nonlocal n
        copy = remote(ref, ref, s9.at[n], r9.at[n], **to)
        copy.start()
        n += 1
        return copy

    first_a = [spread(full.at[0, c, y, x], dx=d) for d in xs]
    first_b = [spread(full.at[1, c, y, x], dy=d) for d in ys]
    for copy in first_a:
        copy.wait_recv()
    second_a = [spread(full.at[0, c, y], dy=d) for d in ys]
    for copy in first_b:
        copy.wait_recv()
    second_b = [spread(full.at[1, c, :, x], dx=d) for d in xs]
    third = [spread(full.at[0, c, y], dc=1), spread(full.at[1, c, :, x], dc=1)]
    for d, copy in zip(ys, second_a):
        copy.wait_recv()
        third.append(spread(full.at[0, c, lax.rem(y + NY - d, NY)], dc=1))
    for d, copy in zip(xs, second_b):
        copy.wait_recv()
        third.append(spread(full.at[1, c, :, lax.rem(x + NX - d, NX)], dc=1))
    for copy in third:
        copy.wait_recv()
    for p in range(2):
        f_hi, f_lo = split(full[p].reshape(n_slots, HALF))
        out_ref[:, HALF * p : HALF * (p + 1)] = dot3(ch[...], cl[...], f_hi, f_lo)
    for group in (sends, stage1, stage2, stage3, stage4, stage5, stage6, first_a, first_b, second_a, second_b, third):
        for copy in group:
            copy.wait_send()


def body(NX, NY, NZ, stop, tokens, slot_params, w_in, w_out):
    T, D = tokens.shape
    n_slots = slot_params.shape[1]
    E, H, _ = w_in.shape
    K = 2 * NY
    padded = -(-T // 128) * 128
    anywhere = pl.BlockSpec(memory_space=pl.ANY)
    vmem = pltpu.VMEM
    dma = pltpu.SemaphoreType.DMA
    scratch = [
        vmem((T, D), F32), vmem((D, n_slots), F32), vmem((E, H, D), F32), vmem((E, H, D), F32),
        vmem((padded, D), BF16), vmem((padded, D), BF16),
        vmem((E, H, D), BF16), vmem((E, H, D), BF16), vmem((E, H, D), BF16), vmem((E, H, D), BF16),
        vmem((padded // 128, n_slots, 128), F32), vmem((n_slots, 128), F32),
        vmem((n_slots, padded), BF16), vmem((n_slots, padded), BF16),
        vmem((T, n_slots), BF16), vmem((T, n_slots), BF16),
        vmem((2, 2, NY, NX, NZ, WIDE), F32), vmem((2, NY, NX, NZ, WIDE), F32), vmem((2, NY, NX, NZ, WIDE), F32),
        vmem((NY - 1, NX, NZ, WIDE), F32), vmem((NX - 1, NY, NZ, WIDE), F32),
        vmem((NX, NZ, WIDE), F32), vmem((NY, NZ, WIDE), F32),
        vmem((NX - 1, NZ, WIDE), F32), vmem((NY - 1, NZ, WIDE), F32),
        vmem((NZ, 1, 2 * WIDE), F32), vmem((NZ, 1, 2 * WIDE), F32),
        vmem((K, 1, D), F32), vmem((K, 1, D), F32), vmem((K - 1, 1, D), F32), vmem((NZ, 1, D), F32),
        vmem((2, 2, NY, NX, NZ, HALF), F32),
    ]
    spreads = 2 * (NX - 1) + 2 * (NY - 1) + NX + NY
    counts = (2, NY - 1, NX - 1, NX - 1, NY - 1, NZ - 1, K - 1, K - 1, NZ - 1, spreads)
    scratch.append(dma((2 * (D // 256) + 2,)))
    for count in counts:
        scratch += [dma((count,)), dma((count,))]
    return pl.pallas_call(
        functools.partial(layer_kernel, NX, NY, NZ, stop),
        out_shape=jax.ShapeDtypeStruct((T, D), F32),
        in_specs=[anywhere] * 4,
        out_specs=pl.BlockSpec(memory_space=pltpu.VMEM),
        scratch_shapes=scratch,
        compiler_params=pltpu.CompilerParams(
            collective_id=0, has_side_effects=True, vmem_limit_bytes=60 * 1024 * 1024
        ),
    )(tokens, slot_params, w_in, w_out)


def solution(mesh, NX=4, NY=4, NZ=8, stop=99):
    torus = Mesh(mesh.devices.reshape(NX, NZ, NY // 2, 2, mesh.shape["fsdp"]), AXES)
    every = ("x", "z", "y_lo", "core", "y_hi")
    return jax.shard_map(
        functools.partial(body, NX, NY, NZ, stop),
        mesh=torus,
        in_specs=(
            P(every, None),
            P(),
            P(("x", "z"), ("y_lo", "core", "y_hi"), None),
            P(("x", "z"), ("y_lo", "core", "y_hi"), None),
        ),
        out_specs=P(every, None),
        check_vma=False,
    )
```

```python
import functools

import jax
import jax.numpy as jnp
from jax import lax
from jax.experimental import pallas as pl
from jax.experimental.pallas import tpu as pltpu
from jax.sharding import Mesh
from jax.sharding import PartitionSpec as P

AXES = ("x", "z", "y_lo", "core", "y_hi")
F32 = jnp.float32
BF16 = jnp.bfloat16
SLOTS = 4
HALF = 640
WIDE = HALF + 128


def split(a):
    hi = a.astype(BF16)
    return hi, (a - hi.astype(F32)).astype(BF16)


TRANSPOSED = (((1,), (1,)), ((), ()))


def dot(a, b, dims=(((1,), (0,)), ((), ()))):
    return lax.dot_general(a, b, dims, preferred_element_type=F32)


def dot3(ah, al, bh, bl, dims=(((1,), (0,)), ((), ()))):
    return dot(ah, bh, dims) + (dot(ah, bl, dims) + dot(al, bh, dims))


def peak_or_mass(peak, mass, rows):
    lane = lax.broadcasted_iota(jnp.int32, (rows, 128), 1)
    return jnp.where(lane < 64, peak, mass)


def merged(parts):
    peaks = [p[:, HALF : HALF + 1] for p in parts]
    peak = functools.reduce(jnp.maximum, peaks)
    total = None
    for part, own in zip(parts, peaks):
        scaled = part * jnp.exp(own - peak)
        total = scaled if total is None else total + scaled
    rows = total.shape[0]
    return total[:, :HALF], peak_or_mass(peak, total[:, HALF + 64 : HALF + 65], rows)


def layer_kernel(
    NX, NY, NZ, stop,
    tok_hbm, par_hbm, win_hbm, wout_hbm, full, ch, cl,
    tok, par, win, wout, xh, xl, wih, wil, woh, wol,
    tmp, ext, wth, wtl, sums, recv_c, kept,
    recv_a, recv_b, two_a, two_b, recv_a2, recv_b2, zsend, zrecv, inputs, osend, orecv, zout,
    ld, sc, rc, s1, r1, s2, r2, s3, r3, s4, r4, s5, r5, s6, r6, s7, r7, s8, r8, s9, r9,
):
    x, z, y_lo, c, y_hi = (lax.axis_index(a) for a in AXES)
    y = y_hi * 2 + y_lo
    tokens, width = tok.shape
    K = 2 * NY
    NXZ = NX * NZ

    def device(dx=0, dy=0, dz=0, dc=0):
        to_y = lax.rem(y + dy, NY)
        return (
            lax.rem(x + dx, NX), lax.rem(z + dz, NZ), lax.rem(to_y, 2),
            lax.rem(c + dc, 2), lax.div(to_y, 2),
        )

    def remote(src, dst, send, recv, **to):
        return pltpu.make_async_remote_copy(
            src_ref=src, dst_ref=dst, send_sem=send, recv_sem=recv,
            device_id=device(**to), device_id_type=pl.DeviceIdType.MESH,
        )

    def put(a):
        for b in range(tmp.shape[0]):
            tmp[b] = a[:, 128 * b : 128 * (b + 1)]

    def every_kth(k):
        return jnp.concatenate([tmp[b, pl.ds(k, NXZ, stride=K), :] for b in range(tmp.shape[0])], axis=1)

    xs, ys, zs = (
        sorted(range(1, n), key=lambda d: -min(d, n - d)) for n in (NX, NY, NZ)
    )
    column = [(dy, dc) for dy in [*ys, 0] for dc in (1, 0) if (dy, dc) != (0, 0)]

    barrier = pltpu.get_barrier_semaphore()
    peers = [dict(dx=d) for d in xs] + [dict(dz=d) for d in zs] + [dict(dy=d, dc=e) for d, e in column]
    for to in peers:
        pl.semaphore_signal(barrier, inc=1, device_id=device(**to), device_id_type=pl.DeviceIdType.MESH)

    steps = width // 256
    loads = []
    for i in range(steps):
        at = pl.ds(256 * i, 256)
        loads.append(pltpu.make_async_copy(tok_hbm.at[:, at], tok.at[:, at], ld.at[2 * i]))
        loads.append(pltpu.make_async_copy(par_hbm.at[at, :], par.at[at, :], ld.at[2 * i + 1]))
    load_win = pltpu.make_async_copy(win_hbm, win, ld.at[2 * steps])
    load_wout = pltpu.make_async_copy(wout_hbm, wout, ld.at[2 * steps + 1])
    for copy in [*loads, load_win, load_wout]:
        copy.start()

    n_slots = par.shape[1]
    pad = xh.shape[0] - tokens
    logits = jnp.zeros((tokens, n_slots), F32)
    for i in range(steps):
        loads[2 * i].wait()
        loads[2 * i + 1].wait()
        at = slice(256 * i, 256 * (i + 1))
        a_hi, a_lo = split(tok[:, at])
        b_hi, b_lo = split(par[at, :])
        xh[0:tokens, at] = a_hi
        xl[0:tokens, at] = a_lo
        logits += dot3(a_hi, a_lo, b_hi, b_lo)
    xh[tokens:, :] = jnp.zeros((pad, width), BF16)
    xl[tokens:, :] = jnp.zeros((pad, width), BF16)

    by_slot = jnp.concatenate([logits, jnp.zeros((pad, n_slots), F32)], axis=0).T
    lane = lax.broadcasted_iota(jnp.int32, by_slot.shape, 1)
    held = lane < tokens
    by_slot = jnp.where(held, by_slot, -3e38)
    peak = jnp.max(by_slot, axis=1, keepdims=True)
    weights = jnp.where(held, jnp.exp(by_slot - peak), 0.0)
    put(weights)
    ext[...] = peak_or_mass(peak, jnp.sum(weights, axis=1, keepdims=True), n_slots)
    for k in range(K):
        row = (k % 2) * (NY * NXZ) + (k // 2) * NXZ
        hi, lo = split(every_kth(k))
        wth[row : row + NXZ, :] = hi
        wtl[row : row + NXZ, :] = lo
        block = ext[pl.ds(k, NXZ, stride=K), :].reshape(NX, NZ, 128)
        for p in range(2):
            sums[p, k % 2, k // 2, :, :, HALF:] = block

    pl.semaphore_wait(barrier, len(peers))
    sends = []
    other = 1 - c
    for p in range(2):
        at = slice(HALF * p, HALF * (p + 1))
        part = dot3(wth[...], wtl[...], xh[:, at], xl[:, at])
        sums[p, :, :, :, :, :HALF] = part.reshape(2, NY, NX, NZ, HALF)
        sends.append(remote(sums.at[p, other], recv_c.at[p], sc.at[p], rc.at[p], dc=1))
        sends[-1].start()

    def fill_weights():
        load_win.wait()
        load_wout.wait()
        wih[...], wil[...] = split(win[...].reshape(wih.shape))
        woh[...], wol[...] = split(wout[...].reshape(woh.shape))

    def fill_combine():
        row_exp = jnp.exp(logits - jnp.max(logits, axis=1, keepdims=True))
        combine = row_exp / jnp.sum(row_exp, axis=1, keepdims=True)
        put(jnp.concatenate([combine, jnp.zeros((pad, n_slots), F32)], axis=0).T)
        order = [every_kth(2 * b + a) for a in range(2) for b in range(NY)]
        ch[...], cl[...] = split(jnp.concatenate(order, axis=0).T[:tokens])

    def flat(a):
        return a.reshape(-1, WIDE)

    def keep(ref, parts):
        total, block = merged([flat(a) for a in parts])
        ref[..., :HALF] = total.reshape(*ref.shape[:-1], HALF)
        ref[..., HALF:] = block.reshape(*ref.shape[:-1], 128)

    sends[0].wait_recv()
    stage1 = []
    for dy in [*ys, 0]:
        to = lax.rem(y + dy, NY)
        keep(kept.at[0, to], [sums[0, c, to], recv_c[0, to]])
        if dy:
            stage1.append(remote(kept.at[0, to], recv_a.at[dy - 1], s1.at[dy - 1], r1.at[dy - 1], dy=dy))
            stage1[-1].start()
    sends[1].wait_recv()
    for dx in [*xs, 0]:
        to = lax.rem(x + dx, NX)
        keep(kept.at[1, :, to], [sums[1, c, :, to], recv_c[1, :, to]])
        if dx:
            stage1.append(remote(kept.at[1, :, to], recv_b.at[dx - 1], s2.at[dx - 1], r2.at[dx - 1], dx=dx))
            stage1[-1].start()
    fill_weights()

    for copy in stage1[: len(ys)]:
        copy.wait_recv()
    keep(two_a, [kept[0, y]] + [recv_a[d] for d in range(NY - 1)])
    stage2 = []
    for dx in xs:
        to = lax.rem(x + dx, NX)
        stage2.append(remote(two_a.at[to], recv_a2.at[dx - 1], s3.at[dx - 1], r3.at[dx - 1], dx=dx))
        stage2[-1].start()
    for copy in stage1[len(ys) :]:
        copy.wait_recv()
    keep(two_b, [kept[1, :, x]] + [recv_b[d] for d in range(NX - 1)])
    for dy in ys:
        to = lax.rem(y + dy, NY)
        stage2.append(remote(two_b.at[to], recv_b2.at[dy - 1], s4.at[dy - 1], r4.at[dy - 1], dy=dy))
        stage2[-1].start()
    fill_combine()

    for copy in stage2:
        copy.wait_recv()
    rows_a = jnp.concatenate(merged([two_a[x]] + [recv_a2[d] for d in range(NX - 1)]), axis=1)
    rows_b = jnp.concatenate(merged([two_b[y]] + [recv_b2[d] for d in range(NY - 1)]), axis=1)
    for i in range(NZ):
        zsend[i, :, :WIDE] = rows_a[i : i + 1]
        zsend[i, :, WIDE:] = rows_b[i : i + 1]
    stage3 = []
    for dz in zs:
        to = lax.rem(z + dz, NZ)
        stage3.append(remote(zsend.at[to], zrecv.at[dz], s5.at[dz - 1], r5.at[dz - 1], dz=dz))
        stage3[-1].start()
    zrecv[0] = zsend[z]
    for copy in stage3:
        copy.wait_recv()
    k = y * 2 + c
    got = zrecv[...].reshape(NZ, 2 * WIDE)
    for p in range(2):
        part = got[:, WIDE * p : WIDE * (p + 1)]
        own = part[:, HALF : HALF + 1]
        total = jnp.sum(part * jnp.exp(own - jnp.max(own, axis=0, keepdims=True)), axis=0, keepdims=True)
        inputs[k, :, HALF * p : HALF * (p + 1)] = total[:, :HALF] / total[:, HALF + 64 : HALF + 65]

    stage4 = []
    for i, (dy, dc) in enumerate(column):
        stage4.append(remote(inputs.at[k], inputs.at[k], s6.at[i], r6.at[i], dy=dy, dc=dc))
        stage4[-1].start()
    for copy in stage4:
        copy.wait_recv()
    s_hi, s_lo = split(inputs[...].reshape(K, width))
    units = wih.shape[0]
    both = dot(jnp.concatenate([s_hi, s_lo], axis=0), wih[...], TRANSPOSED)
    v = both[:K] + (both[K:] + dot(s_hi, wil[...], TRANSPOSED))
    slot = lax.broadcasted_iota(jnp.int32, v.shape, 0)
    unit = lax.broadcasted_iota(jnp.int32, v.shape, 1)
    own = slot // SLOTS == unit // (units // (K // SLOTS))
    hidden = jnp.where(own, v * (1.0 + lax.erf(v * 0.7071067811865476)) * 0.5, 0.0)
    h_hi, h_lo = split(hidden)
    both = dot(jnp.concatenate([h_hi, h_lo], axis=0), woh[...])
    partial = both[:K] + (both[K:] + dot(h_hi, wol[...]))
    for i in range(K):
        osend[i] = partial[i : i + 1]
    stage5 = []
    for i, (dy, dc) in enumerate(column):
        to = lax.rem(y + dy, NY) * 2 + lax.rem(c + dc, 2)
        stage5.append(remote(osend.at[to], orecv.at[i], s7.at[i], r7.at[i], dy=dy, dc=dc))
        stage5[-1].start()
    for copy in stage5:
        copy.wait_recv()
    total = osend[k]
    for i in range(len(column)):
        total += orecv[i]
    zout[z] = total

    stage6 = []
    for dz in zs:
        stage6.append(remote(zout.at[z], zout.at[z], s8.at[dz - 1], r8.at[dz - 1], dz=dz))
        stage6[-1].start()
    for copy in stage6:
        copy.wait_recv()
    rows = zout[...].reshape(NZ, width)
    full[0, c, y, x] = rows[:, :HALF]
    full[1, c, y, x] = rows[:, HALF:]
    stage7 = []
    n = 0

    def spread(ref, **to):
        nonlocal n
        copy = remote(ref, ref, s9.at[n], r9.at[n], **to)
        copy.start()
        n += 1
        return copy

    first_a = [spread(full.at[0, c, y, x], dx=d) for d in xs]
    first_b = [spread(full.at[1, c, y, x], dy=d) for d in ys]
    for copy in first_a:
        copy.wait_recv()
    second_a = [spread(full.at[0, c, y], dy=d) for d in ys]
    for copy in first_b:
        copy.wait_recv()
    second_b = [spread(full.at[1, c, :, x], dx=d) for d in xs]
    third = [spread(full.at[0, c, y], dc=1), spread(full.at[1, c, :, x], dc=1)]
    for d, copy in zip(ys, second_a):
        copy.wait_recv()
        third.append(spread(full.at[0, c, lax.rem(y + NY - d, NY)], dc=1))
    for d, copy in zip(xs, second_b):
        copy.wait_recv()
        third.append(spread(full.at[1, c, :, lax.rem(x + NX - d, NX)], dc=1))
    for copy in third:
        copy.wait_recv()
    for group in (sends, stage1, stage2, stage3, stage4, stage5, stage6, first_a, first_b, second_a, second_b, third):
        for copy in group:
            copy.wait_send()


def mix_kernel(full, ch, cl, out_hbm, out, sem):
    copies = []
    n_slots = ch.shape[1]
    for p in range(2):
        f_hi, f_lo = split(full[p].reshape(n_slots, HALF))
        for start, end in ((0, 256), (256, 512), (512, 640)) if p == 0 else ((0, 128), (128, 384), (384, 640)):
            at = slice(HALF * p + start, HALF * p + end)
            out[:, at] = dot3(ch[...], cl[...], f_hi[:, start:end], f_lo[:, start:end])
            if at.stop % 256 == 0:
                done = pl.ds(at.stop - 256, 256)
                copies.append(pltpu.make_async_copy(out.at[:, done], out_hbm.at[:, done], sem.at[len(copies)]))
                copies[-1].start()
    for copy in copies:
        copy.wait()


def body(NX, NY, NZ, stop, tokens, slot_params, w_in, w_out):
    T, D = tokens.shape
    n_slots = slot_params.shape[1]
    E, H, _ = w_in.shape
    K = 2 * NY
    padded = -(-T // 128) * 128
    anywhere = pl.BlockSpec(memory_space=pltpu.MemorySpace.HBM)
    vmem = pltpu.VMEM
    dma = pltpu.SemaphoreType.DMA
    scratch = [
        vmem((T, D), F32), vmem((D, n_slots), F32), vmem((E, H, D), F32), vmem((E, H, D), F32),
        vmem((padded, D), BF16), vmem((padded, D), BF16),
        vmem((E * H, D), BF16), vmem((E * H, D), BF16), vmem((E * H, D), BF16), vmem((E * H, D), BF16),
        vmem((padded // 128, n_slots, 128), F32), vmem((n_slots, 128), F32),
        vmem((n_slots, padded), BF16), vmem((n_slots, padded), BF16),
        vmem((2, 2, NY, NX, NZ, WIDE), F32), vmem((2, NY, NX, NZ, WIDE), F32), vmem((2, NY, NX, NZ, WIDE), F32),
        vmem((NY - 1, NX, NZ, WIDE), F32), vmem((NX - 1, NY, NZ, WIDE), F32),
        vmem((NX, NZ, WIDE), F32), vmem((NY, NZ, WIDE), F32),
        vmem((NX - 1, NZ, WIDE), F32), vmem((NY - 1, NZ, WIDE), F32),
        vmem((NZ, 1, 2 * WIDE), F32), vmem((NZ, 1, 2 * WIDE), F32),
        vmem((K, 1, D), F32), vmem((K, 1, D), F32), vmem((K - 1, 1, D), F32), vmem((NZ, 1, D), F32),
    ]
    spreads = 2 * (NX - 1) + 2 * (NY - 1) + NX + NY
    counts = (2, NY - 1, NX - 1, NX - 1, NY - 1, NZ - 1, K - 1, K - 1, NZ - 1, spreads)
    scratch.append(dma((2 * (D // 256) + 2,)))
    for count in counts:
        scratch += [dma((count,)), dma((count,))]
    args = [pltpu.with_memory_space_constraint(a, pltpu.MemorySpace.HBM) for a in (tokens, slot_params, w_in, w_out)]
    full, ch, cl = pl.pallas_call(
        functools.partial(layer_kernel, NX, NY, NZ, stop),
        out_shape=(
            jax.ShapeDtypeStruct((2, 2, NY, NX, NZ, HALF), F32),
            jax.ShapeDtypeStruct((T, n_slots), BF16),
            jax.ShapeDtypeStruct((T, n_slots), BF16),
        ),
        in_specs=[anywhere] * 4,
        out_specs=(pl.BlockSpec(memory_space=pltpu.VMEM),) * 3,
        scratch_shapes=scratch,
        compiler_params=pltpu.CompilerParams(
            collective_id=0, has_side_effects=True, vmem_limit_bytes=40 * 1024 * 1024
        ),
        name="layer",
    )(*args)
    return pl.pallas_call(
        mix_kernel,
        out_shape=jax.ShapeDtypeStruct((T, D), F32),
        in_specs=[pl.BlockSpec(memory_space=pltpu.VMEM)] * 3,
        out_specs=anywhere,
        scratch_shapes=[vmem((T, D), F32), dma((D // 256,))],
        compiler_params=pltpu.CompilerParams(vmem_limit_bytes=16 * 1024 * 1024),
        name="mix",
    )(full, ch, cl)


def solution(mesh, NX=4, NY=4, NZ=8, stop=99):
    torus = Mesh(mesh.devices.reshape(NX, NZ, NY // 2, 2, mesh.shape["fsdp"]), AXES)
    every = ("x", "z", "y_lo", "core", "y_hi")
    return jax.shard_map(
        functools.partial(body, NX, NY, NZ, stop),
        mesh=torus,
        in_specs=(
            P(every, None),
            P(),
            P(("x", "z"), ("y_lo", "core", "y_hi"), None),
            P(("x", "z"), ("y_lo", "core", "y_hi"), None),
        ),
        out_specs=P(every, None),
        check_vma=False,
    )
```

```python
import functools

import jax
import jax.numpy as jnp
from jax import lax
from jax.experimental import pallas as pl
from jax.experimental.pallas import tpu as pltpu
from jax.sharding import Mesh
from jax.sharding import PartitionSpec as P

AXES = ("x", "z", "y_lo", "core", "y_hi")
F32 = jnp.float32
BF16 = jnp.bfloat16
SLOTS = 4
HALF = 640
WIDE = HALF + 128


def split(a):
    hi = a.astype(BF16)
    return hi, (a - hi.astype(F32)).astype(BF16)


TRANSPOSED = (((1,), (1,)), ((), ()))


def dot(a, b, dims=(((1,), (0,)), ((), ()))):
    return lax.dot_general(a, b, dims, preferred_element_type=F32)


def dot3(ah, al, bh, bl):
    return dot(ah, bh) + (dot(ah, bl) + dot(al, bh))


def peak_or_mass(peak, mass, rows):
    lane = lax.broadcasted_iota(jnp.int32, (rows, 128), 1)
    return jnp.where(lane < 64, peak, mass)


def merged(parts):
    peaks = [p[:, HALF : HALF + 1] for p in parts]
    peak = functools.reduce(jnp.maximum, peaks)
    total = None
    for part, own in zip(parts, peaks):
        scaled = part * jnp.exp(own - peak)
        total = scaled if total is None else total + scaled
    rows = total.shape[0]
    return total[:, :HALF], peak_or_mass(peak, total[:, HALF + 64 : HALF + 65], rows)


def layer_kernel(
    NX, NY, NZ, stop,
    tok_hbm, par_hbm, win_hbm, wout_hbm, full, ch, cl,
    tok, par, win, wout, xh, xl, wih, wil, woh, wol,
    tmp, ext, wth, wtl, sums, recv_c, kept,
    recv_a, recv_b, rows_a, rows_b, got_a, got_b, inputs, osend, orecv, own_out, all_a, all_b,
    ld, sent, came,
):
    x, z, y_lo, c, y_hi = (lax.axis_index(a) for a in AXES)
    y = y_hi * 2 + y_lo
    tokens, width = tok.shape
    K = 2 * NY
    NXZ = NX * NZ

    def device(dx=0, dy=0, dz=0, dc=0):
        to_y = lax.rem(y + dy, NY)
        return (
            lax.rem(x + dx, NX), lax.rem(z + dz, NZ), lax.rem(to_y, 2),
            lax.rem(c + dc, 2), lax.div(to_y, 2),
        )

    def remote(src, dst, group, arrival=None, **to):
        return pltpu.make_async_remote_copy(
            src_ref=src, dst_ref=dst, send_sem=sent.at[group], recv_sem=came.at[group if arrival is None else arrival],
            device_id=device(**to), device_id_type=pl.DeviceIdType.MESH,
        )

    def put(a):
        for b in range(tmp.shape[0]):
            tmp[b] = a[:, 128 * b : 128 * (b + 1)]

    def every_kth(k):
        return jnp.concatenate([tmp[b, pl.ds(k, NXZ, stride=K), :] for b in range(tmp.shape[0])], axis=1)

    def hops(d, n):
        return min(d, n - d)

    xs, ys = (sorted(range(1, n), key=lambda d: -hops(d, n)) for n in (NX, NY))
    whole = []

    def one_wait(group, ref):
        copy = remote(ref, ref, group, dc=1)
        copy.wait_recv()
        whole.append(copy)

    column = [(dy, dc) for dy in [*ys, 0] for dc in (1, 0) if (dy, dc) != (0, 0)]
    plane_a, plane_b = (
        sorted(
            ((d, dz) for d in range(n) for dz in range(NZ) if (d, dz) != (0, 0)),
            key=lambda to: -hops(to[0], n) - hops(to[1], NZ),
        )
        for n in (NX, NY)
    )

    steps = width // 256
    loads = []
    for i in range(steps):
        at = pl.ds(256 * i, 256)
        loads.append(pltpu.make_async_copy(tok_hbm.at[:, at], tok.at[:, at], ld.at[2 * i]))
        loads.append(pltpu.make_async_copy(par_hbm.at[at, :], par.at[at, :], ld.at[2 * i + 1]))
    load_win = pltpu.make_async_copy(win_hbm, win, ld.at[2 * steps])
    load_wout = pltpu.make_async_copy(wout_hbm, wout, ld.at[2 * steps + 1])
    for copy in [*loads, load_win, load_wout]:
        copy.start()

    barrier = pltpu.get_barrier_semaphore()
    peers = [dict(dc=1)] + [dict(dx=d) for d in xs] + [dict(dy=d) for d in ys] + [dict(dz=d) for d in range(1, NZ)]
    for to in peers:
        pl.semaphore_signal(barrier, inc=1, device_id=device(**to), device_id_type=pl.DeviceIdType.MESH)

    n_slots = par.shape[1]
    pad = xh.shape[0] - tokens
    logits = jnp.zeros((tokens, n_slots), F32)
    for i in range(steps):
        loads[2 * i].wait()
        loads[2 * i + 1].wait()
        at = slice(256 * i, 256 * (i + 1))
        a_hi, a_lo = split(tok[:, at])
        b_hi, b_lo = split(par[at, :])
        xh[0:tokens, at] = a_hi
        xl[0:tokens, at] = a_lo
        logits += dot3(a_hi, a_lo, b_hi, b_lo)
    xh[tokens:, :] = jnp.zeros((pad, width), BF16)
    xl[tokens:, :] = jnp.zeros((pad, width), BF16)

    by_slot = jnp.concatenate([logits, jnp.zeros((pad, n_slots), F32)], axis=0).T
    lane = lax.broadcasted_iota(jnp.int32, by_slot.shape, 1)
    held = lane < tokens
    by_slot = jnp.where(held, by_slot, -3e38)
    peak = jnp.max(by_slot, axis=1, keepdims=True)
    weights = jnp.where(held, jnp.exp(by_slot - peak), 0.0)
    put(weights)
    ext[...] = peak_or_mass(peak, jnp.sum(weights, axis=1, keepdims=True), n_slots)
    for k in range(K):
        row = (k % 2) * (NY * NXZ) + (k // 2) * NXZ
        hi, lo = split(every_kth(k))
        wth[row : row + NXZ, :] = hi
        wtl[row : row + NXZ, :] = lo
        block = ext[pl.ds(k, NXZ, stride=K), :].reshape(NX, NZ, 128)
        for p in range(2):
            sums[p, k % 2, k // 2, :, :, HALF:] = block

    sends = []
    other = 1 - c
    for p in range(2):
        at = slice(HALF * p, HALF * (p + 1))
        part = dot3(wth[...], wtl[...], xh[:, at], xl[:, at])
        sums[p, :, :, :, :, :HALF] = part.reshape(2, NY, NX, NZ, HALF)
        if p == 0:
            pl.semaphore_wait(barrier, len(peers))
        sends.append(remote(sums.at[p, other], recv_c.at[p], p, dc=1))
        sends[-1].start()

    def fill_weights():
        load_win.wait()
        load_wout.wait()
        wih[...], wil[...] = split(win[...].reshape(wih.shape))
        woh[...], wol[...] = split(wout[...].reshape(woh.shape))

    def fill_combine():
        row_exp = jnp.exp(logits - jnp.max(logits, axis=1, keepdims=True))
        combine = row_exp / jnp.sum(row_exp, axis=1, keepdims=True)
        put(jnp.concatenate([combine, jnp.zeros((pad, n_slots), F32)], axis=0).T)
        order = [every_kth(2 * b + a) for a in range(2) for b in range(NY)]
        ch[...], cl[...] = split(jnp.concatenate(order, axis=0).T[:tokens])

    def flat(a):
        return a.reshape(-1, WIDE)

    def keep(ref, parts):
        total, block = merged([flat(a) for a in parts])
        ref[..., :HALF] = total.reshape(*ref.shape[:-1], HALF)
        ref[..., HALF:] = block.reshape(*ref.shape[:-1], 128)

    sends[0].wait_recv()
    for dy in ys:
        to = lax.rem(y + dy, NY)
        keep(kept.at[0, to], [sums[0, c, to], recv_c[0, to]])
        remote(kept.at[0, to], recv_a.at[dy - 1], 2, dy=dy).start()
    sends[1].wait_recv()
    for dx in xs:
        to = lax.rem(x + dx, NX)
        keep(kept.at[1, :, to], [sums[1, c, :, to], recv_c[1, :, to]])
        remote(kept.at[1, :, to], recv_b.at[dx - 1], 3, dx=dx).start()
    keep(kept.at[0, y], [sums[0, c, y], recv_c[0, y]])
    keep(kept.at[1, :, x], [sums[1, c, :, x], recv_c[1, :, x]])
    fill_weights()

    def to_owners(rows, own, received, got, group, plane, n, at, axis):
        total, block = merged([flat(a) for a in [own, *received]])
        total = jnp.concatenate([total, block], axis=1)
        for i in range(n * NZ):
            rows[i // NZ, i % NZ] = total[i : i + 1]
        for d, dz in plane:
            src = rows.at[lax.rem(at + d, n), lax.rem(z + dz, NZ)]
            remote(src, got.at[d * NZ + dz], group, **{axis: d}, dz=dz).start()
        got[0] = rows[at, z]

    one_wait(2, recv_a)
    one_wait(3, recv_b)
    to_owners(rows_a, kept[0, y], [recv_a[d] for d in range(NY - 1)], got_a, 4, plane_a, NX, x, "dx")
    to_owners(rows_b, kept[1, :, x], [recv_b[d] for d in range(NX - 1)], got_b, 5, plane_b, NY, y, "dy")
    fill_combine()

    one_wait(4, got_a.at[1:])
    one_wait(5, got_b.at[1:])
    k = y * 2 + c
    for p, got in enumerate((got_a, got_b)):
        part = got[...].reshape(-1, WIDE)
        own = part[:, HALF : HALF + 1]
        total = jnp.sum(part * jnp.exp(own - jnp.max(own, axis=0, keepdims=True)), axis=0, keepdims=True)
        inputs[k, :, HALF * p : HALF * (p + 1)] = total[:, :HALF] / total[:, HALF + 64 : HALF + 65]

    for dy, dc in column:
        remote(inputs.at[k], inputs.at[k], 6, dy=dy, dc=dc).start()
    one_wait(6, inputs.at[1:])
    s_hi, s_lo = split(inputs[...].reshape(K, width))
    units = wih.shape[0]
    both = dot(jnp.concatenate([s_hi, s_lo], axis=0), wih[...], TRANSPOSED)
    v = both[:K] + (both[K:] + dot(s_hi, wil[...], TRANSPOSED))
    slot = lax.broadcasted_iota(jnp.int32, v.shape, 0)
    unit = lax.broadcasted_iota(jnp.int32, v.shape, 1)
    own = slot // SLOTS == unit // (units // (K // SLOTS))
    hidden = jnp.where(own, v * (1.0 + lax.erf(v * 0.7071067811865476)) * 0.5, 0.0)
    h_hi, h_lo = split(hidden)
    both = dot(jnp.concatenate([h_hi, h_lo], axis=0), woh[...])
    partial = both[:K] + (both[K:] + dot(h_hi, wol[...]))
    for i in range(K):
        osend[i] = partial[i : i + 1]
    for i, (dy, dc) in enumerate(column):
        to = lax.rem(y + dy, NY) * 2 + lax.rem(c + dc, 2)
        remote(osend.at[to], orecv.at[i], 7, dy=dy, dc=dc).start()
    one_wait(7, orecv)
    total = osend[k]
    for i in range(len(column)):
        total += orecv[i]
    own_out[0] = total[:, :HALF]
    own_out[1] = total[:, HALF:]

    def to_plane(src, everything, group, plane, at, axis):
        row = at * NZ + z
        for d, dz in plane:
            remote(src, everything.at[row], group, **{axis: d}, dz=dz).start()
        everything[row] = src[...]

    to_plane(own_out.at[0], all_a, 8, plane_a, x, "dx")
    to_plane(own_out.at[1], all_b, 9, plane_b, y, "dy")

    def block(p, d=0):
        if p == 0:
            return full.at[0, c, lax.rem(y + NY - d, NY)]
        return full.at[1, c, :, lax.rem(x + NX - d, NX)]

    def spread(p, ds, axis):
        copies = {}
        for d in ds:
            copies[d] = remote(block(p), block(p), 10 + p, 10 + 3 * p + d, **{axis: d})
            copies[d].start()
        remote(block(p), block(p), 12, 17, dc=1).start()
        return copies

    one_wait(8, all_a.at[1:])
    full[0, c, y] = all_a[...].reshape(NX, NZ, HALF)
    last_a = spread(0, ys, "dy")
    one_wait(9, all_b.at[1:])
    full[1, c, :, x] = all_b[...].reshape(NY, NZ, HALF)
    last_b = spread(1, xs, "dx")
    for d in reversed(ys):
        last_a[d].wait_recv()
        remote(block(0, d), block(0, d), 12, 17, dc=1).start()
    for d in reversed(xs):
        last_b[d].wait_recv()
        remote(block(1, d), block(1, d), 12, 17, dc=1).start()
    theirs = full.at[:, other]
    remote(theirs, theirs, 12, 17, dc=1).wait()
    for copy in sends + whole:
        copy.wait_send()
    three_a, three_b = full.at[0, c, 1:], full.at[1, c, :, 1:]
    remote(three_a, three_a, 10, dc=1).wait_send()
    remote(three_b, three_b, 11, dc=1).wait_send()


def mix_kernel(full, ch, cl, out_hbm, out, sem):
    copies = []
    n_slots = ch.shape[1]
    for p in range(2):
        f_hi, f_lo = split(full[p].reshape(n_slots, HALF))
        for start, end in ((0, 256), (256, 512), (512, 640)) if p == 0 else ((0, 128), (128, 384), (384, 640)):
            at = slice(HALF * p + start, HALF * p + end)
            out[:, at] = dot3(ch[...], cl[...], f_hi[:, start:end], f_lo[:, start:end])
            if at.stop % 256 == 0:
                done = pl.ds(at.stop - 256, 256)
                copies.append(pltpu.make_async_copy(out.at[:, done], out_hbm.at[:, done], sem.at[len(copies)]))
                copies[-1].start()
    for copy in copies:
        copy.wait()


def body(NX, NY, NZ, stop, tokens, slot_params, w_in, w_out):
    T, D = tokens.shape
    n_slots = slot_params.shape[1]
    E, H, _ = w_in.shape
    K = 2 * NY
    padded = -(-T // 128) * 128
    anywhere = pl.BlockSpec(memory_space=pltpu.MemorySpace.HBM)
    vmem = pltpu.VMEM
    dma = pltpu.SemaphoreType.DMA
    scratch = [
        vmem((T, D), F32), vmem((D, n_slots), F32), vmem((E, H, D), F32), vmem((E, H, D), F32),
        vmem((padded, D), BF16), vmem((padded, D), BF16),
        vmem((E * H, D), BF16), vmem((E * H, D), BF16), vmem((E * H, D), BF16), vmem((E * H, D), BF16),
        vmem((padded // 128, n_slots, 128), F32), vmem((n_slots, 128), F32),
        vmem((n_slots, padded), BF16), vmem((n_slots, padded), BF16),
        vmem((2, 2, NY, NX, NZ, WIDE), F32), vmem((2, NY, NX, NZ, WIDE), F32), vmem((2, NY, NX, NZ, WIDE), F32),
        vmem((NY - 1, NX, NZ, WIDE), F32), vmem((NX - 1, NY, NZ, WIDE), F32),
        vmem((NX, NZ, 1, WIDE), F32), vmem((NY, NZ, 1, WIDE), F32),
        vmem((NX * NZ, 1, WIDE), F32), vmem((NY * NZ, 1, WIDE), F32),
        vmem((K, 1, D), F32), vmem((K, 1, D), F32), vmem((K - 1, 1, D), F32), vmem((2, 1, HALF), F32),
        vmem((NX * NZ, 1, HALF), F32), vmem((NY * NZ, 1, HALF), F32),
    ]
    scratch += [dma((2 * (D // 256) + 2,)), dma((13,)), dma((18,))]
    args = [pltpu.with_memory_space_constraint(a, pltpu.MemorySpace.HBM) for a in (tokens, slot_params, w_in, w_out)]
    full, ch, cl = pl.pallas_call(
        functools.partial(layer_kernel, NX, NY, NZ, stop),
        out_shape=(
            jax.ShapeDtypeStruct((2, 2, NY, NX, NZ, HALF), F32),
            jax.ShapeDtypeStruct((T, n_slots), BF16),
            jax.ShapeDtypeStruct((T, n_slots), BF16),
        ),
        in_specs=[anywhere] * 4,
        out_specs=(pl.BlockSpec(memory_space=pltpu.VMEM),) * 3,
        scratch_shapes=scratch,
        compiler_params=pltpu.CompilerParams(
            collective_id=0, has_side_effects=True, vmem_limit_bytes=40 * 1024 * 1024
        ),
        name="layer",
    )(*args)
    return pl.pallas_call(
        mix_kernel,
        out_shape=jax.ShapeDtypeStruct((T, D), F32),
        in_specs=[pl.BlockSpec(memory_space=pltpu.VMEM)] * 3,
        out_specs=anywhere,
        scratch_shapes=[vmem((T, D), F32), dma((D // 256,))],
        compiler_params=pltpu.CompilerParams(vmem_limit_bytes=16 * 1024 * 1024),
        name="mix",
    )(full, ch, cl)


def solution(mesh, NX=4, NY=4, NZ=8, stop=99):
    torus = Mesh(mesh.devices.reshape(NX, NZ, NY // 2, 2, mesh.shape["fsdp"]), AXES)
    every = ("x", "z", "y_lo", "core", "y_hi")
    return jax.shard_map(
        functools.partial(body, NX, NY, NZ, stop),
        mesh=torus,
        in_specs=(
            P(every, None),
            P(),
            P(("x", "z"), ("y_lo", "core", "y_hi"), None),
            P(("x", "z"), ("y_lo", "core", "y_hi"), None),
        ),
        out_specs=P(every, None),
        check_vma=False,
    )
```

```python
import functools

import jax
import jax.numpy as jnp
from jax import lax
from jax.experimental import pallas as pl
from jax.experimental.pallas import tpu as pltpu
from jax.sharding import Mesh
from jax.sharding import PartitionSpec as P

AXES = ("x", "z", "y_lo", "core", "y_hi")
F32 = jnp.float32
BF16 = jnp.bfloat16
SLOTS = 4
HALF = 640
FIRST = 768
WIDE = HALF + 128


def split(a):
    hi = a.astype(BF16)
    return hi, (a - hi.astype(F32)).astype(BF16)


def dot(a, b):
    return jnp.dot(a, b, preferred_element_type=F32)


def dot3(ah, al, bh, bl):
    return dot(ah, bh) + (dot(ah, bl) + dot(al, bh))


def peak_or_mass(peak, mass, rows):
    lane = lax.broadcasted_iota(jnp.int32, (rows, 128), 1)
    return jnp.where(lane < 64, peak, mass)


def unpacked(a):
    return a[:, :HALF], a[:, HALF : HALF + 1], a[:, HALF + 64 : HALF + 65]


def merged(parts):
    top = functools.reduce(jnp.maximum, [peak for _, peak, _ in parts])
    scales = [jnp.exp(peak - top) for _, peak, _ in parts]
    total = sum(part * scale for (part, _, _), scale in zip(parts, scales))
    return total, top, sum(mass * scale for (_, _, mass), scale in zip(parts, scales))


def group_lanes(groups, rows):
    lane = lax.broadcasted_iota(jnp.int32, (rows, 128), 1)
    return lane, 64 // groups


def layer_kernel(
    NX, NY, NZ, stop,
    tok_hbm, par_hbm, win_hbm, wout_hbm, their_a, their_b, mixed, ch, cl,
    tok, par, win, wout, xh, xl, wih, wil, woh, wol,
    tmp, ext, wth, wtl, sums, recv_c, kept, notes_a, notes_b, came_a, came_b,
    recv_a, recv_b, rows_a, rows_b, got_a, got_b, inputs, osend, orecv, out_a, out_b, all_a, all_b, own_a, own_b, oh, ol,
    ld, sent, came,
):
    x, z, y_lo, c, y_hi = (lax.axis_index(a) for a in AXES)
    y = y_hi * 2 + y_lo
    tokens, width = tok.shape
    K = 2 * NY
    NXZ = NX * NZ

    def device(dx=0, dy=0, dz=0, dc=0):
        to_y = lax.rem(y + dy, NY)
        return (
            lax.rem(x + dx, NX), lax.rem(z + dz, NZ), lax.rem(to_y, 2),
            lax.rem(c + dc, 2), lax.div(to_y, 2),
        )

    def remote(src, dst, group, arrival=None, **to):
        return pltpu.make_async_remote_copy(
            src_ref=src, dst_ref=dst, send_sem=sent.at[group], recv_sem=came.at[group if arrival is None else arrival],
            device_id=device(**to), device_id_type=pl.DeviceIdType.MESH,
        )

    def put(a):
        for b in range(tmp.shape[0]):
            tmp[b] = a[:, 128 * b : 128 * (b + 1)]

    def every_kth(k):
        return jnp.concatenate([tmp[b, pl.ds(k, NXZ, stride=K), :] for b in range(tmp.shape[0])], axis=1)

    def hops(d, n):
        return min(d, n - d)

    xs, ys = (sorted(range(1, n), key=lambda d: -hops(d, n)) for n in (NX, NY))
    whole = []

    def one_wait(group, ref, arrival=None):
        copy = remote(ref, ref, group, arrival, dc=1)
        copy.wait_recv()
        whole.append(copy)

    column = [(dy, dc) for dy in [*ys, 0] for dc in (1, 0) if (dy, dc) != (0, 0)]
    plane_a, plane_b = (
        sorted(
            ((d, dz) for d in range(n) for dz in range(NZ) if (d, dz) != (0, 0)),
            key=lambda to: -hops(to[0], n) - hops(to[1], NZ),
        )
        for n in (NX, NY)
    )

    steps = width // 256
    loads = []
    for i in range(steps):
        at = pl.ds(256 * i, 256)
        loads.append(pltpu.make_async_copy(tok_hbm.at[:, at], tok.at[:, at], ld.at[2 * i]))
        loads.append(pltpu.make_async_copy(par_hbm.at[at, :], par.at[at, :], ld.at[2 * i + 1]))
    load_win = pltpu.make_async_copy(win_hbm, win, ld.at[2 * steps])
    load_wout = pltpu.make_async_copy(wout_hbm, wout, ld.at[2 * steps + 1])
    for copy in [*loads, load_win, load_wout]:
        copy.start()

    barrier = pltpu.get_barrier_semaphore()
    peers = [dict(dc=1)] + [dict(dx=d) for d in xs] + [dict(dy=d) for d in ys] + [dict(dz=d) for d in range(1, NZ)]
    for to in peers:
        pl.semaphore_signal(barrier, inc=1, device_id=device(**to), device_id_type=pl.DeviceIdType.MESH)

    n_slots = par.shape[1]
    pad = xh.shape[0] - tokens
    logits = jnp.zeros((tokens, n_slots), F32)
    for i in range(steps):
        loads[2 * i].wait()
        loads[2 * i + 1].wait()
        at = slice(256 * i, 256 * (i + 1))
        a_hi, a_lo = split(tok[:, at])
        b_hi, b_lo = split(par[at, :])
        xh[0:tokens, at] = a_hi
        xl[0:tokens, at] = a_lo
        logits += dot3(a_hi, a_lo, b_hi, b_lo)
    xh[tokens:, :] = jnp.zeros((pad, width), BF16)
    xl[tokens:, :] = jnp.zeros((pad, width), BF16)

    by_slot = jnp.concatenate([logits, jnp.zeros((pad, n_slots), F32)], axis=0).T
    lane = lax.broadcasted_iota(jnp.int32, by_slot.shape, 1)
    held = lane < tokens
    by_slot = jnp.where(held, by_slot, -3e38)
    peak = jnp.max(by_slot, axis=1, keepdims=True)
    weights = jnp.where(held, jnp.exp(by_slot - peak), 0.0)
    put(weights)
    ext[...] = peak_or_mass(peak, jnp.sum(weights, axis=1, keepdims=True), n_slots)
    for k in range(K):
        row = (k % 2) * (NY * NXZ) + (k // 2) * NXZ
        hi, lo = split(every_kth(k))
        wth[row : row + NXZ, :] = hi
        wtl[row : row + NXZ, :] = lo
        block = ext[pl.ds(k, NXZ, stride=K), :].reshape(NX, NZ, 128)
        for p in range(2):
            sums[p, k % 2, k // 2, :, :, HALF:] = block

    sends = []
    other = 1 - c
    for p in range(2):
        at = slice(HALF * p, HALF * (p + 1))
        part = dot3(wth[...], wtl[...], xh[:, at], xl[:, at])
        sums[p, :, :, :, :, :HALF] = part.reshape(2, NY, NX, NZ, HALF)
        if p == 0:
            pl.semaphore_wait(barrier, len(peers))
        sends.append(remote(sums.at[p, other], recv_c.at[p], p, dc=1))
        sends[-1].start()

    def fill_weights():
        load_win.wait()
        load_wout.wait()
        wih[...], wil[...] = split(win[...].reshape(woh.shape).T)
        woh[...], wol[...] = split(wout[...].reshape(woh.shape))

    def fill_combine():
        row_exp = jnp.exp(logits - jnp.max(logits, axis=1, keepdims=True))
        combine = row_exp / jnp.sum(row_exp, axis=1, keepdims=True)
        put(jnp.concatenate([combine, jnp.zeros((pad, n_slots), F32)], axis=0).T)
        order = [every_kth(2 * b + a) for a in range(2) for b in range(NY)]
        by_token = jnp.concatenate(order, axis=0).T[:tokens]
        first, second = by_token[:, : n_slots // 2], by_token[:, n_slots // 2 :]
        oh[...], ol[...] = split(jnp.where(c == 0, first, second))
        ch[...], cl[...] = split(jnp.where(c == 0, second, first))

    def flat(a):
        return a.reshape(-1, a.shape[-1])

    def joined(p, at):
        return merged([unpacked(flat(sums[(p, c, *at)])), unpacked(flat(recv_c[(p, *at)]))])

    def keep(ref, notes, triple):
        total, peak, mass = triple
        ref[...] = total.reshape(ref.shape)
        groups = total.shape[0] // NZ
        lane, wide = group_lanes(groups, NZ)
        block = None
        for g in range(groups):
            rows = slice(g * NZ, (g + 1) * NZ)
            own = jnp.where(lane < 64, peak[rows], mass[rows])
            block = own if g == 0 else jnp.where(lane % 64 // wide == g, own, block)
        notes[...] = block

    def noted(ref, notes):
        total, block = flat(ref[...]), notes[...]
        groups = total.shape[0] // NZ
        wide = 64 // groups
        peak, mass = (
            jnp.concatenate([block[:, at + wide * g : at + wide * g + 1] for g in range(groups)], axis=0)
            for at in (0, 64)
        )
        return total, peak, mass

    sends[0].wait_recv()
    for dy in reversed(ys):
        to = lax.rem(y + dy, NY)
        keep(kept.at[0, to], notes_a.at[to], joined(0, (to,)))
        remote(notes_a.at[to], came_a.at[dy - 1], 13, 18, dy=dy).start()
        remote(kept.at[0, to], recv_a.at[dy - 1], 2, dy=dy).start()
    sends[1].wait_recv()
    for dx in reversed(xs):
        to = lax.rem(x + dx, NX)
        keep(kept.at[1, :, to], notes_b.at[to], joined(1, (slice(None), to)))
        remote(notes_b.at[to], came_b.at[dx - 1], 14, 19, dx=dx).start()
        remote(kept.at[1, :, to], recv_b.at[dx - 1], 3, dx=dx).start()
    keep(kept.at[0, y], notes_a.at[y], joined(0, (y,)))
    keep(kept.at[1, :, x], notes_b.at[x], joined(1, (slice(None), x)))
    fill_weights()

    def to_owners(rows, parts, got, group, plane, n, at, axis):
        total, peak, mass = merged(parts)
        total = jnp.concatenate([total, peak_or_mass(peak, mass, n * NZ)], axis=1)
        for i in range(n * NZ):
            rows[i // NZ, i % NZ] = total[i : i + 1]
        for d, dz in plane:
            src = rows.at[lax.rem(at + d, n), lax.rem(z + dz, NZ)]
            remote(src, got.at[d * NZ + dz], group, **{axis: d}, dz=dz).start()
        got[0] = rows[at, z]

    one_wait(13, came_a, 18)
    one_wait(2, recv_a)
    one_wait(14, came_b, 19)
    one_wait(3, recv_b)
    parts = [noted(kept.at[0, y], notes_a.at[y])] + [noted(recv_a.at[d], came_a.at[d]) for d in range(NY - 1)]
    to_owners(rows_a, parts, got_a, 4, plane_a, NX, x, "dx")
    parts = [noted(kept.at[1, :, x], notes_b.at[x])] + [noted(recv_b.at[d], came_b.at[d]) for d in range(NX - 1)]
    to_owners(rows_b, parts, got_b, 5, plane_b, NY, y, "dy")
    fill_combine()

    one_wait(4, got_a.at[1:])
    one_wait(5, got_b.at[1:])
    k = y * 2 + c
    for p, got in enumerate((got_a, got_b)):
        total, peak, mass = unpacked(got[...].reshape(-1, WIDE))
        scale = jnp.exp(peak - jnp.max(peak, axis=0, keepdims=True))
        total, mass = (jnp.sum(a * scale, axis=0, keepdims=True) for a in (total, mass))
        inputs[k, :, HALF * p : HALF * (p + 1)] = total / mass

    for dy, dc in column:
        remote(inputs.at[k], inputs.at[k], 6, dy=dy, dc=dc).start()
    one_wait(6, inputs.at[1:])
    s_hi, s_lo = split(inputs[...].reshape(K, width))
    units = wih.shape[1]
    both = dot(jnp.concatenate([s_hi, s_lo], axis=0), wih[...])
    v = both[:K] + (both[K:] + dot(s_hi, wil[...]))
    slot = lax.broadcasted_iota(jnp.int32, v.shape, 0)
    unit = lax.broadcasted_iota(jnp.int32, v.shape, 1)
    own = slot // SLOTS == unit // (units // (K // SLOTS))
    hidden = jnp.where(own, v * (1.0 + lax.erf(v * 0.7071067811865476)) * 0.5, 0.0)
    h_hi, h_lo = split(hidden)
    both = dot(jnp.concatenate([h_hi, h_lo], axis=0), woh[...])
    partial = both[:K] + (both[K:] + dot(h_hi, wol[...]))
    for i in range(K):
        osend[i] = partial[i : i + 1]
    for i, (dy, dc) in enumerate(column):
        to = lax.rem(y + dy, NY) * 2 + lax.rem(c + dc, 2)
        remote(osend.at[to], orecv.at[i], 7, dy=dy, dc=dc).start()
    one_wait(7, orecv)
    total = osend[k]
    for i in range(len(column)):
        total += orecv[i]
    out_a[...] = total[:, :FIRST]
    out_b[...] = total[:, FIRST:]

    def to_plane(src, everything, group, plane, at, axis):
        row = at * NZ + z
        for d, dz in plane:
            remote(src, everything.at[row], group, **{axis: d}, dz=dz).start()
        everything[row] = src[...]

    to_plane(out_a, all_a, 8, plane_a, x, "dx")
    to_plane(out_b, all_b, 9, plane_b, y, "dy")

    def block(p, d, own=True):
        if p == 0:
            return (own_a if own else their_a).at[lax.rem(y + NY - d, NY)]
        return (own_b if own else their_b).at[:, lax.rem(x + NX - d, NX)]

    def pass_on(p, d):
        remote(block(p, d), block(p, d, False), 12 + 3 * p, 17 + 3 * p, dc=1).start()

    def spread(p, ds, axis):
        copies = {}
        for d in ds:
            copies[d] = remote(block(p, 0), block(p, 0), 10 + p, 10 + 3 * p + d, **{axis: d})
            copies[d].start()
        pass_on(p, 0)
        return copies

    one_wait(8, all_a.at[1:])
    own_a[y] = all_a[...].reshape(NX, NZ, FIRST)
    last_a = spread(0, ys, "dy")
    one_wait(9, all_b.at[1:])
    own_b[:, x] = all_b[...].reshape(NY, NZ, own_b.shape[-1])
    last_b = spread(1, xs, "dx")
    for d in reversed(ys):
        last_a[d].wait_recv()
        pass_on(0, d)
    for d in reversed(xs):
        last_b[d].wait_recv()
        pass_on(1, d)
    mixed[:, :FIRST] = dot3(oh[...], ol[...], *split(flat(own_a[...])))
    mixed[:, FIRST:] = dot3(oh[...], ol[...], *split(flat(own_b[...])))
    one_wait(12, their_a, 17)
    one_wait(15, their_b, 20)
    for copy in sends + whole:
        copy.wait_send()
    three_a, three_b = own_a.at[1:], own_b.at[:, 1:]
    remote(three_a, three_a, 10, dc=1).wait_send()
    remote(three_b, three_b, 11, dc=1).wait_send()


def mix_kernel(their_a, their_b, mixed, ch, cl, out_hbm, out, sem):
    copies = []
    start = 0
    for part in (their_a, their_b):
        f_hi, f_lo = split(part[...].reshape(-1, part.shape[-1]))
        for i in range(0, part.shape[-1], 256):
            at = slice(start + i, start + i + 256)
            out[:, at] = mixed[:, at] + dot3(ch[...], cl[...], f_hi[:, i : i + 256], f_lo[:, i : i + 256])
            done = pl.ds(at.start, 256)
            copies.append(pltpu.make_async_copy(out.at[:, done], out_hbm.at[:, done], sem.at[len(copies)]))
            copies[-1].start()
        start += part.shape[-1]
    for copy in copies:
        copy.wait()


def body(NX, NY, NZ, stop, tokens, slot_params, w_in, w_out):
    T, D = tokens.shape
    n_slots = slot_params.shape[1]
    E, H, _ = w_in.shape
    K = 2 * NY
    padded = -(-T // 128) * 128
    anywhere = pl.BlockSpec(memory_space=pltpu.MemorySpace.HBM)
    vmem = pltpu.VMEM
    dma = pltpu.SemaphoreType.DMA
    scratch = [
        vmem((T, D), F32), vmem((D, n_slots), F32), vmem((E, H, D), F32), vmem((E, H, D), F32),
        vmem((padded, D), BF16), vmem((padded, D), BF16),
        vmem((D, E * H), BF16), vmem((D, E * H), BF16), vmem((E * H, D), BF16), vmem((E * H, D), BF16),
        vmem((padded // 128, n_slots, 128), F32), vmem((n_slots, 128), F32),
        vmem((n_slots, padded), BF16), vmem((n_slots, padded), BF16),
        vmem((2, 2, NY, NX, NZ, WIDE), F32), vmem((2, NY, NX, NZ, WIDE), F32), vmem((2, NY, NX, NZ, HALF), F32),
        vmem((NY, NZ, 128), F32), vmem((NX, NZ, 128), F32), vmem((NY - 1, NZ, 128), F32), vmem((NX - 1, NZ, 128), F32),
        vmem((NY - 1, NX, NZ, HALF), F32), vmem((NX - 1, NY, NZ, HALF), F32),
        vmem((NX, NZ, 1, WIDE), F32), vmem((NY, NZ, 1, WIDE), F32),
        vmem((NX * NZ, 1, WIDE), F32), vmem((NY * NZ, 1, WIDE), F32),
        vmem((K, 1, D), F32), vmem((K, 1, D), F32), vmem((K - 1, 1, D), F32), vmem((1, FIRST), F32), vmem((1, D - FIRST), F32),
        vmem((NX * NZ, 1, FIRST), F32), vmem((NY * NZ, 1, D - FIRST), F32),
        vmem((NY, NX, NZ, FIRST), F32), vmem((NY, NX, NZ, D - FIRST), F32),
        vmem((T, n_slots // 2), BF16), vmem((T, n_slots // 2), BF16),
    ]
    scratch += [dma((2 * (D // 256) + 2,)), dma((16,)), dma((21,))]
    args = [pltpu.with_memory_space_constraint(a, pltpu.MemorySpace.HBM) for a in (tokens, slot_params, w_in, w_out)]
    results = pl.pallas_call(
        functools.partial(layer_kernel, NX, NY, NZ, stop),
        out_shape=(
            jax.ShapeDtypeStruct((NY, NX, NZ, FIRST), F32),
            jax.ShapeDtypeStruct((NY, NX, NZ, D - FIRST), F32),
            jax.ShapeDtypeStruct((T, D), F32),
            jax.ShapeDtypeStruct((T, n_slots // 2), BF16),
            jax.ShapeDtypeStruct((T, n_slots // 2), BF16),
        ),
        in_specs=[anywhere] * 4,
        out_specs=(pl.BlockSpec(memory_space=pltpu.VMEM),) * 5,
        scratch_shapes=scratch,
        compiler_params=pltpu.CompilerParams(
            collective_id=0, has_side_effects=True, vmem_limit_bytes=40 * 1024 * 1024
        ),
        name="layer",
    )(*args)
    return pl.pallas_call(
        mix_kernel,
        out_shape=jax.ShapeDtypeStruct((T, D), F32),
        in_specs=[pl.BlockSpec(memory_space=pltpu.VMEM)] * 5,
        out_specs=anywhere,
        scratch_shapes=[vmem((T, D), F32), dma((D // 256,))],
        compiler_params=pltpu.CompilerParams(vmem_limit_bytes=16 * 1024 * 1024),
        name="mix",
    )(*results)


def solution(mesh, NX=4, NY=4, NZ=8, stop=99):
    torus = Mesh(mesh.devices.reshape(NX, NZ, NY // 2, 2, mesh.shape["fsdp"]), AXES)
    every = ("x", "z", "y_lo", "core", "y_hi")
    return jax.shard_map(
        functools.partial(body, NX, NY, NZ, stop),
        mesh=torus,
        in_specs=(
            P(every, None),
            P(),
            P(("x", "z"), ("y_lo", "core", "y_hi"), None),
            P(("x", "z"), ("y_lo", "core", "y_hi"), None),
        ),
        out_specs=P(every, None),
        check_vma=False,
    )
```

```python
import functools

import jax
import jax.numpy as jnp
from jax import lax
from jax.experimental import pallas as pl
from jax.experimental.pallas import tpu as pltpu
from jax.sharding import Mesh
from jax.sharding import PartitionSpec as P

AXES = ("x", "z", "y_lo", "core", "y_hi")
F32 = jnp.float32
BF16 = jnp.bfloat16
SLOTS = 4
HALF = 640
FIRST = 768
WIDE = HALF + 128


def split(a):
    hi = a.astype(BF16)
    return hi, (a - hi.astype(F32)).astype(BF16)


def dot(a, b):
    return jnp.dot(a, b, preferred_element_type=F32)


def dot3(ah, al, bh, bl):
    return dot(ah, bh) + (dot(ah, bl) + dot(al, bh))


def peak_or_mass(peak, mass, rows):
    lane = lax.broadcasted_iota(jnp.int32, (rows, 128), 1)
    return jnp.where(lane < 64, peak, mass)


def unpacked(a):
    return a[:, :HALF], a[:, HALF : HALF + 1], a[:, HALF + 64 : HALF + 65]


def merged(parts):
    top = functools.reduce(jnp.maximum, [peak for _, peak, _ in parts])
    scales = [jnp.exp(peak - top) for _, peak, _ in parts]
    total = sum(part * scale for (part, _, _), scale in zip(parts, scales))
    return total, top, sum(mass * scale for (_, _, mass), scale in zip(parts, scales))


def group_lanes(groups, rows):
    lane = lax.broadcasted_iota(jnp.int32, (rows, 128), 1)
    return lane, 64 // groups


def layer_kernel(
    NX, NY, NZ, stop,
    tok_hbm, par_hbm, win_hbm, wout_hbm, their_a, their_b, mixed, ch, cl,
    tok, par, win, wout, xh, xl, wih, wil, woh, wol,
    tmp, ext, wth, wtl, sums, recv_c, kept, scales, notes_a, notes_b, came_a, came_b,
    recv_a, recv_b, rows_a, rows_b, got_a, got_b, inputs, osend, orecv, out_a, out_b, all_a, all_b, own_a, own_b, oh, ol,
    ld, sent, came,
):
    x, z, y_lo, c, y_hi = (lax.axis_index(a) for a in AXES)
    y = y_hi * 2 + y_lo
    tokens, width = tok.shape
    K = 2 * NY
    NXZ = NX * NZ

    def device(dx=0, dy=0, dz=0, dc=0):
        to_y = lax.rem(y + dy, NY)
        return (
            lax.rem(x + dx, NX), lax.rem(z + dz, NZ), lax.rem(to_y, 2),
            lax.rem(c + dc, 2), lax.div(to_y, 2),
        )

    def remote(src, dst, group, arrival=None, **to):
        return pltpu.make_async_remote_copy(
            src_ref=src, dst_ref=dst, send_sem=sent.at[group], recv_sem=came.at[group if arrival is None else arrival],
            device_id=device(**to), device_id_type=pl.DeviceIdType.MESH,
        )

    def put(a):
        for b in range(tmp.shape[0]):
            tmp[b] = a[:, 128 * b : 128 * (b + 1)]

    def every_kth(k):
        return jnp.concatenate([tmp[b, pl.ds(k, NXZ, stride=K), :] for b in range(tmp.shape[0])], axis=1)

    def hops(d, n):
        return min(d, n - d)

    xs, ys = (sorted(range(1, n), key=lambda d: -hops(d, n)) for n in (NX, NY))
    whole = []

    def one_wait(group, ref, arrival=None):
        copy = remote(ref, ref, group, arrival, dc=1)
        copy.wait_recv()
        whole.append(copy)

    column = [(dy, dc) for dy in [*ys, 0] for dc in (1, 0) if (dy, dc) != (0, 0)]
    plane_a, plane_b = (
        sorted(
            ((d, dz) for d in range(n) for dz in range(NZ) if (d, dz) != (0, 0)),
            key=lambda to: -hops(to[0], n) - hops(to[1], NZ),
        )
        for n in (NX, NY)
    )

    steps = width // 256
    loads = []
    for i in range(steps):
        at = pl.ds(256 * i, 256)
        loads.append(pltpu.make_async_copy(tok_hbm.at[:, at], tok.at[:, at], ld.at[2 * i]))
        loads.append(pltpu.make_async_copy(par_hbm.at[at, :], par.at[at, :], ld.at[2 * i + 1]))
    load_win = pltpu.make_async_copy(win_hbm, win, ld.at[2 * steps])
    load_wout = pltpu.make_async_copy(wout_hbm, wout, ld.at[2 * steps + 1])
    for copy in [*loads, load_win, load_wout]:
        copy.start()

    barrier = pltpu.get_barrier_semaphore()
    peers = [dict(dc=1)] + [dict(dx=d) for d in xs] + [dict(dy=d) for d in ys] + [dict(dz=d) for d in range(1, NZ)]
    for to in peers:
        pl.semaphore_signal(barrier, inc=1, device_id=device(**to), device_id_type=pl.DeviceIdType.MESH)

    n_slots = par.shape[1]
    pad = xh.shape[0] - tokens
    logits = jnp.zeros((tokens, n_slots), F32)
    for i in range(steps):
        loads[2 * i].wait()
        loads[2 * i + 1].wait()
        at = slice(256 * i, 256 * (i + 1))
        a_hi, a_lo = split(tok[:, at])
        b_hi, b_lo = split(par[at, :])
        xh[0:tokens, at] = a_hi
        xl[0:tokens, at] = a_lo
        logits += dot3(a_hi, a_lo, b_hi, b_lo)
    xh[tokens:, :] = jnp.zeros((pad, width), BF16)
    xl[tokens:, :] = jnp.zeros((pad, width), BF16)

    by_slot = jnp.concatenate([logits, jnp.zeros((pad, n_slots), F32)], axis=0).T
    lane = lax.broadcasted_iota(jnp.int32, by_slot.shape, 1)
    held = lane < tokens
    by_slot = jnp.where(held, by_slot, -3e38)
    peak = jnp.max(by_slot, axis=1, keepdims=True)
    weights = jnp.where(held, jnp.exp(by_slot - peak), 0.0)
    put(weights)
    ext[...] = peak_or_mass(peak, jnp.sum(weights, axis=1, keepdims=True), n_slots)
    for k in range(K):
        row = (k % 2) * (NY * NXZ) + (k // 2) * NXZ
        hi, lo = split(every_kth(k))
        wth[row : row + NXZ, :] = hi
        wtl[row : row + NXZ, :] = lo
        block = ext[pl.ds(k, NXZ, stride=K), :].reshape(NX, NZ, 128)
        for p in range(2):
            sums[p, k % 2, k // 2, :, :, HALF:] = block

    sends = []
    other = 1 - c
    for p in range(2):
        at = slice(HALF * p, HALF * (p + 1))
        part = dot3(wth[...], wtl[...], xh[:, at], xl[:, at])
        sums[p, :, :, :, :, :HALF] = part.reshape(2, NY, NX, NZ, HALF)
        if p == 0:
            pl.semaphore_wait(barrier, len(peers))
        sends.append(remote(sums.at[p, other], recv_c.at[p], p, dc=1))
        sends[-1].start()

    def fill_weights():
        load_win.wait()
        load_wout.wait()
        wih[...], wil[...] = split(win[...].reshape(woh.shape).T)
        woh[...], wol[...] = split(wout[...].reshape(woh.shape))

    def fill_combine():
        row_exp = jnp.exp(logits - jnp.max(logits, axis=1, keepdims=True))
        combine = row_exp / jnp.sum(row_exp, axis=1, keepdims=True)
        put(jnp.concatenate([combine, jnp.zeros((pad, n_slots), F32)], axis=0).T)
        order = [every_kth(2 * b + a) for a in range(2) for b in range(NY)]
        by_token = jnp.concatenate(order, axis=0).T[:tokens]
        first, second = by_token[:, : n_slots // 2], by_token[:, n_slots // 2 :]
        oh[...], ol[...] = split(jnp.where(c == 0, first, second))
        ch[...], cl[...] = split(jnp.where(c == 0, second, first))

    def flat(a):
        return a.reshape(-1, a.shape[-1])

    def packed(blocks):
        lane, wide = group_lanes(len(blocks), NZ)
        packet = blocks[0]
        for g, own in enumerate(blocks):
            packet = jnp.where(lane % 64 // wide == g, own, packet)
        return packet

    def fill_scales():
        ours, theirs = flat(sums[0, c, :, :, :, HALF:]), flat(recv_c[0, :, :, :, HALF:])
        top = jnp.maximum(ours[:, :1], theirs[:, :1])
        mass = None
        for i, part in enumerate((ours, theirs)):
            scale = jnp.exp(part[:, :1] - top)
            scales[i] = jnp.broadcast_to(scale, part.shape).reshape(NY, NX, NZ, 128)
            own = part[:, 64:65] * scale
            mass = own if mass is None else mass + own
        block = peak_or_mass(top, mass, top.shape[0])
        tiles = [[block[(yi * NX + xi) * NZ : (yi * NX + xi + 1) * NZ] for xi in range(NX)] for yi in range(NY)]
        for yi in range(NY):
            notes_a[yi] = packed(tiles[yi])
        for xi in range(NX):
            notes_b[xi] = packed([tiles[yi][xi] for yi in range(NY)])

    def keep(p, *at):
        both = (sums[(p, c, *at)], recv_c[(p, *at)])
        scaled = [a[..., :HALF] * jnp.concatenate([scales[(i, *at)]] * (HALF // 128), axis=-1) for i, a in enumerate(both)]
        kept[(p, *at)] = scaled[0] + scaled[1]

    def noted(ref, notes):
        total, block = flat(ref[...]), notes[...]
        groups = total.shape[0] // NZ
        wide = 64 // groups
        peak, mass = (
            jnp.concatenate([block[:, at + wide * g : at + wide * g + 1] for g in range(groups)], axis=0)
            for at in (0, 64)
        )
        return total, peak, mass

    sends[0].wait_recv()
    fill_scales()
    for dy in reversed(ys):
        to = lax.rem(y + dy, NY)
        remote(notes_a.at[to], came_a.at[dy - 1], 13, 18, dy=dy).start()
    for dx in reversed(xs):
        to = lax.rem(x + dx, NX)
        remote(notes_b.at[to], came_b.at[dx - 1], 14, 19, dx=dx).start()
    for dy in reversed(ys):
        to = lax.rem(y + dy, NY)
        keep(0, to)
        remote(kept.at[0, to], recv_a.at[dy - 1], 2, dy=dy).start()
    sends[1].wait_recv()
    for dx in reversed(xs):
        to = lax.rem(x + dx, NX)
        keep(1, slice(None), to)
        remote(kept.at[1, :, to], recv_b.at[dx - 1], 3, dx=dx).start()
    keep(0, y)
    keep(1, slice(None), x)
    fill_weights()

    def to_owners(rows, parts, got, group, plane, n, at, axis):
        total, peak, mass = merged(parts)
        total = jnp.concatenate([total, peak_or_mass(peak, mass, n * NZ)], axis=1)
        for i in range(n * NZ):
            rows[i // NZ, i % NZ] = total[i : i + 1]
        for d, dz in plane:
            src = rows.at[lax.rem(at + d, n), lax.rem(z + dz, NZ)]
            remote(src, got.at[d * NZ + dz], group, **{axis: d}, dz=dz).start()
        got[0] = rows[at, z]

    one_wait(13, came_a, 18)
    one_wait(14, came_b, 19)
    one_wait(2, recv_a)
    parts = [noted(kept.at[0, y], notes_a.at[y])] + [noted(recv_a.at[d], came_a.at[d]) for d in range(NY - 1)]
    to_owners(rows_a, parts, got_a, 4, plane_a, NX, x, "dx")
    one_wait(3, recv_b)
    parts = [noted(kept.at[1, :, x], notes_b.at[x])] + [noted(recv_b.at[d], came_b.at[d]) for d in range(NX - 1)]
    to_owners(rows_b, parts, got_b, 5, plane_b, NY, y, "dy")
    fill_combine()

    one_wait(4, got_a.at[1:])
    one_wait(5, got_b.at[1:])
    k = y * 2 + c
    for p, got in enumerate((got_a, got_b)):
        total, peak, mass = unpacked(got[...].reshape(-1, WIDE))
        scale = jnp.exp(peak - jnp.max(peak, axis=0, keepdims=True))
        total, mass = (jnp.sum(a * scale, axis=0, keepdims=True) for a in (total, mass))
        inputs[k, :, HALF * p : HALF * (p + 1)] = total / mass

    for dy, dc in column:
        remote(inputs.at[k], inputs.at[k], 6, dy=dy, dc=dc).start()
    one_wait(6, inputs.at[1:])
    s_hi, s_lo = split(inputs[...].reshape(K, width))
    units = wih.shape[1]
    both = dot(jnp.concatenate([s_hi, s_lo], axis=0), wih[...])
    v = both[:K] + (both[K:] + dot(s_hi, wil[...]))
    slot = lax.broadcasted_iota(jnp.int32, v.shape, 0)
    unit = lax.broadcasted_iota(jnp.int32, v.shape, 1)
    own = slot // SLOTS == unit // (units // (K // SLOTS))
    hidden = jnp.where(own, v * (1.0 + lax.erf(v * 0.7071067811865476)) * 0.5, 0.0)
    h_hi, h_lo = split(hidden)
    both = dot(jnp.concatenate([h_hi, h_lo], axis=0), woh[...])
    partial = both[:K] + (both[K:] + dot(h_hi, wol[...]))
    for i in range(K):
        osend[i] = partial[i : i + 1]
    for i, (dy, dc) in enumerate(column):
        to = lax.rem(y + dy, NY) * 2 + lax.rem(c + dc, 2)
        remote(osend.at[to], orecv.at[i], 7, dy=dy, dc=dc).start()
    one_wait(7, orecv)
    total = osend[k]
    for i in range(len(column)):
        total += orecv[i]
    out_a[...] = total[:, :FIRST]
    out_b[...] = total[:, FIRST:]

    def to_plane(src, everything, group, plane, at, axis):
        row = at * NZ + z
        for d, dz in plane:
            remote(src, everything.at[row], group, **{axis: d}, dz=dz).start()
        everything[row] = src[...]

    to_plane(out_a, all_a, 8, plane_a, x, "dx")
    to_plane(out_b, all_b, 9, plane_b, y, "dy")

    def block(p, d, own=True):
        if p == 0:
            return (own_a if own else their_a).at[lax.rem(y + NY - d, NY)]
        return (own_b if own else their_b).at[:, lax.rem(x + NX - d, NX)]

    def pass_on(p, d):
        remote(block(p, d), block(p, d, False), 12 + 3 * p, 17 + 3 * p, dc=1).start()

    def spread(p, ds, axis):
        copies = {}
        for d in ds:
            copies[d] = remote(block(p, 0), block(p, 0), 10 + p, 10 + 3 * p + d, **{axis: d})
            copies[d].start()
        pass_on(p, 0)
        return copies

    one_wait(8, all_a.at[1:])
    own_a[y] = all_a[...].reshape(NX, NZ, FIRST)
    last_a = spread(0, ys, "dy")
    one_wait(9, all_b.at[1:])
    own_b[:, x] = all_b[...].reshape(NY, NZ, own_b.shape[-1])
    last_b = spread(1, xs, "dx")
    for d in reversed(ys):
        last_a[d].wait_recv()
        pass_on(0, d)
    for d in reversed(xs):
        last_b[d].wait_recv()
        pass_on(1, d)
    mixed[:, :FIRST] = dot3(oh[...], ol[...], *split(flat(own_a[...])))
    mixed[:, FIRST:] = dot3(oh[...], ol[...], *split(flat(own_b[...])))
    one_wait(12, their_a, 17)
    one_wait(15, their_b, 20)
    for copy in sends + whole:
        copy.wait_send()
    three_a, three_b = own_a.at[1:], own_b.at[:, 1:]
    remote(three_a, three_a, 10, dc=1).wait_send()
    remote(three_b, three_b, 11, dc=1).wait_send()


def mix_kernel(their_a, their_b, mixed, ch, cl, out_hbm, out, sem):
    copies = []
    start = 0
    for part in (their_a, their_b):
        f_hi, f_lo = split(part[...].reshape(-1, part.shape[-1]))
        for i in range(0, part.shape[-1], 256):
            at = slice(start + i, start + i + 256)
            out[:, at] = mixed[:, at] + dot3(ch[...], cl[...], f_hi[:, i : i + 256], f_lo[:, i : i + 256])
            done = pl.ds(at.start, 256)
            copies.append(pltpu.make_async_copy(out.at[:, done], out_hbm.at[:, done], sem.at[len(copies)]))
            copies[-1].start()
        start += part.shape[-1]
    for copy in copies:
        copy.wait()


def body(NX, NY, NZ, stop, tokens, slot_params, w_in, w_out):
    T, D = tokens.shape
    n_slots = slot_params.shape[1]
    E, H, _ = w_in.shape
    K = 2 * NY
    padded = -(-T // 128) * 128
    anywhere = pl.BlockSpec(memory_space=pltpu.MemorySpace.HBM)
    vmem = pltpu.VMEM
    dma = pltpu.SemaphoreType.DMA
    scratch = [
        vmem((T, D), F32), vmem((D, n_slots), F32), vmem((E, H, D), F32), vmem((E, H, D), F32),
        vmem((padded, D), BF16), vmem((padded, D), BF16),
        vmem((D, E * H), BF16), vmem((D, E * H), BF16), vmem((E * H, D), BF16), vmem((E * H, D), BF16),
        vmem((padded // 128, n_slots, 128), F32), vmem((n_slots, 128), F32),
        vmem((n_slots, padded), BF16), vmem((n_slots, padded), BF16),
        vmem((2, 2, NY, NX, NZ, WIDE), F32), vmem((2, NY, NX, NZ, WIDE), F32), vmem((2, NY, NX, NZ, HALF), F32), vmem((2, NY, NX, NZ, 128), F32),
        vmem((NY, NZ, 128), F32), vmem((NX, NZ, 128), F32), vmem((NY - 1, NZ, 128), F32), vmem((NX - 1, NZ, 128), F32),
        vmem((NY - 1, NX, NZ, HALF), F32), vmem((NX - 1, NY, NZ, HALF), F32),
        vmem((NX, NZ, 1, WIDE), F32), vmem((NY, NZ, 1, WIDE), F32),
        vmem((NX * NZ, 1, WIDE), F32), vmem((NY * NZ, 1, WIDE), F32),
        vmem((K, 1, D), F32), vmem((K, 1, D), F32), vmem((K - 1, 1, D), F32), vmem((1, FIRST), F32), vmem((1, D - FIRST), F32),
        vmem((NX * NZ, 1, FIRST), F32), vmem((NY * NZ, 1, D - FIRST), F32),
        vmem((NY, NX, NZ, FIRST), F32), vmem((NY, NX, NZ, D - FIRST), F32),
        vmem((T, n_slots // 2), BF16), vmem((T, n_slots // 2), BF16),
    ]
    scratch += [dma((2 * (D // 256) + 2,)), dma((16,)), dma((21,))]
    args = [pltpu.with_memory_space_constraint(a, pltpu.MemorySpace.HBM) for a in (tokens, slot_params, w_in, w_out)]
    results = pl.pallas_call(
        functools.partial(layer_kernel, NX, NY, NZ, stop),
        out_shape=(
            jax.ShapeDtypeStruct((NY, NX, NZ, FIRST), F32),
            jax.ShapeDtypeStruct((NY, NX, NZ, D - FIRST), F32),
            jax.ShapeDtypeStruct((T, D), F32),
            jax.ShapeDtypeStruct((T, n_slots // 2), BF16),
            jax.ShapeDtypeStruct((T, n_slots // 2), BF16),
        ),
        in_specs=[anywhere] * 4,
        out_specs=(pl.BlockSpec(memory_space=pltpu.VMEM),) * 5,
        scratch_shapes=scratch,
        compiler_params=pltpu.CompilerParams(
            collective_id=0, has_side_effects=True, vmem_limit_bytes=40 * 1024 * 1024
        ),
        name="layer",
    )(*args)
    return pl.pallas_call(
        mix_kernel,
        out_shape=jax.ShapeDtypeStruct((T, D), F32),
        in_specs=[pl.BlockSpec(memory_space=pltpu.VMEM)] * 5,
        out_specs=anywhere,
        scratch_shapes=[vmem((T, D), F32), dma((D // 256,))],
        compiler_params=pltpu.CompilerParams(vmem_limit_bytes=16 * 1024 * 1024),
        name="mix",
    )(*results)


def solution(mesh, NX=4, NY=4, NZ=8, stop=99):
    torus = Mesh(mesh.devices.reshape(NX, NZ, NY // 2, 2, mesh.shape["fsdp"]), AXES)
    every = ("x", "z", "y_lo", "core", "y_hi")
    return jax.shard_map(
        functools.partial(body, NX, NY, NZ, stop),
        mesh=torus,
        in_specs=(
            P(every, None),
            P(),
            P(("x", "z"), ("y_lo", "core", "y_hi"), None),
            P(("x", "z"), ("y_lo", "core", "y_hi"), None),
        ),
        out_specs=P(every, None),
        check_vma=False,
    )
```

```python
import functools

import jax
import jax.numpy as jnp
from jax import lax
from jax.experimental import pallas as pl
from jax.experimental.pallas import tpu as pltpu
from jax.sharding import Mesh
from jax.sharding import PartitionSpec as P

AXES = ("x", "z", "y_lo", "core", "y_hi")
F32 = jnp.float32
BF16 = jnp.bfloat16
SLOTS = 4
HALF = 640
FIRST = 768
WIDE = HALF + 128


def split(a):
    hi = a.astype(BF16)
    return hi, (a - hi.astype(F32)).astype(BF16)


def dot(a, b):
    return jnp.dot(a, b, preferred_element_type=F32)


def dot3(ah, al, bh, bl):
    return dot(ah, bh) + (dot(ah, bl) + dot(al, bh))


def peak_or_mass(peak, mass, rows):
    lane = lax.broadcasted_iota(jnp.int32, (rows, 128), 1)
    return jnp.where(lane < 64, peak, mass)


def unpacked(a):
    return a[:, :HALF], a[:, HALF : HALF + 1], a[:, HALF + 64 : HALF + 65]


def merged(parts):
    top = functools.reduce(jnp.maximum, [peak for _, peak, _ in parts])
    scales = [jnp.exp(peak - top) for _, peak, _ in parts]
    total = sum(part * scale for (part, _, _), scale in zip(parts, scales))
    return total, top, sum(mass * scale for (_, _, mass), scale in zip(parts, scales))


def group_lanes(groups, rows):
    lane = lax.broadcasted_iota(jnp.int32, (rows, 128), 1)
    return lane, 64 // groups


def layer_kernel(
    NX, NY, NZ, stop,
    tok_hbm, par_hbm, win_hbm, wout_hbm, their_b, mixed, ch, cl,
    tok, par, win, wout, xh, xl, wih, wil, woh, wol,
    tmp, ext, wth, wtl, sums, recv_c, kept, scales, notes_a, notes_b, came_a, came_b,
    recv_a, recv_b, rows_a, rows_b, got_a, got_b, inputs, osend, orecv, out_a, out_b, all_a, all_b, own_a, own_b, their_a, oh, ol,
    ld, sent, came,
):
    x, z, y_lo, c, y_hi = (lax.axis_index(a) for a in AXES)
    y = y_hi * 2 + y_lo
    tokens, width = tok.shape
    K = 2 * NY
    NXZ = NX * NZ

    def device(dx=0, dy=0, dz=0, dc=0):
        to_y = lax.rem(y + dy, NY)
        return (
            lax.rem(x + dx, NX), lax.rem(z + dz, NZ), lax.rem(to_y, 2),
            lax.rem(c + dc, 2), lax.div(to_y, 2),
        )

    def remote(src, dst, group, arrival=None, **to):
        return pltpu.make_async_remote_copy(
            src_ref=src, dst_ref=dst, send_sem=sent.at[group], recv_sem=came.at[group if arrival is None else arrival],
            device_id=device(**to), device_id_type=pl.DeviceIdType.MESH,
        )

    def put(a):
        for b in range(tmp.shape[0]):
            tmp[b] = a[:, 128 * b : 128 * (b + 1)]

    def every_kth(k):
        return jnp.concatenate([tmp[b, pl.ds(k, NXZ, stride=K), :] for b in range(tmp.shape[0])], axis=1)

    def hops(d, n):
        return min(d, n - d)

    xs, ys = (sorted(range(1, n), key=lambda d: -hops(d, n)) for n in (NX, NY))
    whole = []

    def one_wait(group, ref, arrival=None):
        copy = remote(ref, ref, group, arrival, dc=1)
        copy.wait_recv()
        whole.append(copy)

    column = [(dy, dc) for dy in [*ys, 0] for dc in (1, 0) if (dy, dc) != (0, 0)]
    plane_a, plane_b = (
        sorted(
            ((d, dz) for d in range(n) for dz in range(NZ) if (d, dz) != (0, 0)),
            key=lambda to: -hops(to[0], n) - hops(to[1], NZ),
        )
        for n in (NX, NY)
    )

    steps = width // 256
    loads = []
    for i in range(steps):
        at = pl.ds(256 * i, 256)
        loads.append(pltpu.make_async_copy(tok_hbm.at[:, at], tok.at[:, at], ld.at[2 * i]))
        loads.append(pltpu.make_async_copy(par_hbm.at[at, :], par.at[at, :], ld.at[2 * i + 1]))
    load_win = pltpu.make_async_copy(win_hbm, win, ld.at[2 * steps])
    load_wout = pltpu.make_async_copy(wout_hbm, wout, ld.at[2 * steps + 1])
    for copy in [*loads, load_win, load_wout]:
        copy.start()

    barrier = pltpu.get_barrier_semaphore()
    peers = [dict(dc=1)] + [dict(dx=d) for d in xs] + [dict(dy=d) for d in ys] + [dict(dz=d) for d in range(1, NZ)]
    for to in peers:
        pl.semaphore_signal(barrier, inc=1, device_id=device(**to), device_id_type=pl.DeviceIdType.MESH)

    n_slots = par.shape[1]
    pad = xh.shape[0] - tokens
    logits = jnp.zeros((tokens, n_slots), F32)
    for i in range(steps):
        loads[2 * i].wait()
        loads[2 * i + 1].wait()
        at = slice(256 * i, 256 * (i + 1))
        a_hi, a_lo = split(tok[:, at])
        b_hi, b_lo = split(par[at, :])
        xh[0:tokens, at] = a_hi
        xl[0:tokens, at] = a_lo
        logits += dot3(a_hi, a_lo, b_hi, b_lo)
    xh[tokens:, :] = jnp.zeros((pad, width), BF16)
    xl[tokens:, :] = jnp.zeros((pad, width), BF16)

    by_slot = jnp.concatenate([logits, jnp.zeros((pad, n_slots), F32)], axis=0).T
    lane = lax.broadcasted_iota(jnp.int32, by_slot.shape, 1)
    held = lane < tokens
    by_slot = jnp.where(held, by_slot, -3e38)
    peak = jnp.max(by_slot, axis=1, keepdims=True)
    weights = jnp.where(held, jnp.exp(by_slot - peak), 0.0)
    put(weights)
    ext[...] = peak_or_mass(peak, jnp.sum(weights, axis=1, keepdims=True), n_slots)
    for k in range(K):
        row = (k % 2) * (NY * NXZ) + (k // 2) * NXZ
        hi, lo = split(every_kth(k))
        wth[row : row + NXZ, :] = hi
        wtl[row : row + NXZ, :] = lo
        block = ext[pl.ds(k, NXZ, stride=K), :].reshape(NX, NZ, 128)
        for p in range(2):
            sums[p, k % 2, k // 2, :, :, HALF:] = block

    sends = []
    other = 1 - c
    for p in range(2):
        at = slice(HALF * p, HALF * (p + 1))
        part = dot3(wth[...], wtl[...], xh[:, at], xl[:, at])
        sums[p, :, :, :, :, :HALF] = part.reshape(2, NY, NX, NZ, HALF)
        if p == 0:
            pl.semaphore_wait(barrier, len(peers))
        sends.append(remote(sums.at[p, other], recv_c.at[p], p, dc=1))
        sends[-1].start()

    def fill_weights():
        load_win.wait()
        load_wout.wait()
        wih[...], wil[...] = split(win[...].reshape(woh.shape).T)
        woh[...], wol[...] = split(wout[...].reshape(woh.shape))

    def fill_combine():
        row_exp = jnp.exp(logits - jnp.max(logits, axis=1, keepdims=True))
        combine = row_exp / jnp.sum(row_exp, axis=1, keepdims=True)
        put(jnp.concatenate([combine, jnp.zeros((pad, n_slots), F32)], axis=0).T)
        order = [every_kth(2 * b + a) for a in range(2) for b in range(NY)]
        by_token = jnp.concatenate(order, axis=0).T[:tokens]
        first, second = by_token[:, : n_slots // 2], by_token[:, n_slots // 2 :]
        oh[...], ol[...] = split(jnp.where(c == 0, first, second))
        ch[...], cl[...] = split(jnp.where(c == 0, second, first))

    def flat(a):
        return a.reshape(-1, a.shape[-1])

    def packed(blocks):
        lane, wide = group_lanes(len(blocks), NZ)
        packet = blocks[0]
        for g, own in enumerate(blocks):
            packet = jnp.where(lane % 64 // wide == g, own, packet)
        return packet

    def fill_scales():
        ours, theirs = flat(sums[0, c, :, :, :, HALF:]), flat(recv_c[0, :, :, :, HALF:])
        top = jnp.maximum(ours[:, :1], theirs[:, :1])
        mass = None
        for i, part in enumerate((ours, theirs)):
            scale = jnp.exp(part[:, :1] - top)
            scales[i] = jnp.broadcast_to(scale, part.shape).reshape(NY, NX, NZ, 128)
            own = part[:, 64:65] * scale
            mass = own if mass is None else mass + own
        block = peak_or_mass(top, mass, top.shape[0])
        tiles = [[block[(yi * NX + xi) * NZ : (yi * NX + xi + 1) * NZ] for xi in range(NX)] for yi in range(NY)]
        for yi in range(NY):
            notes_a[yi] = packed(tiles[yi])
        for xi in range(NX):
            notes_b[xi] = packed([tiles[yi][xi] for yi in range(NY)])

    def keep(p, *at):
        both = (sums[(p, c, *at)], recv_c[(p, *at)])
        scaled = [a[..., :HALF] * jnp.concatenate([scales[(i, *at)]] * (HALF // 128), axis=-1) for i, a in enumerate(both)]
        kept[(p, *at)] = scaled[0] + scaled[1]

    def noted(ref, notes):
        total, block = flat(ref[...]), notes[...]
        groups = total.shape[0] // NZ
        wide = 64 // groups
        peak, mass = (
            jnp.concatenate([block[:, at + wide * g : at + wide * g + 1] for g in range(groups)], axis=0)
            for at in (0, 64)
        )
        return total, peak, mass

    sends[0].wait_recv()
    fill_scales()
    for dy in reversed(ys):
        to = lax.rem(y + dy, NY)
        remote(notes_a.at[to], came_a.at[dy - 1], 13, 18, dy=dy).start()
    for dx in reversed(xs):
        to = lax.rem(x + dx, NX)
        remote(notes_b.at[to], came_b.at[dx - 1], 14, 19, dx=dx).start()
    for dy in reversed(ys):
        to = lax.rem(y + dy, NY)
        keep(0, to)
        remote(kept.at[0, to], recv_a.at[dy - 1], 2, dy=dy).start()
    sends[1].wait_recv()
    for dx in reversed(xs):
        to = lax.rem(x + dx, NX)
        keep(1, slice(None), to)
        remote(kept.at[1, :, to], recv_b.at[dx - 1], 3, dx=dx).start()
    keep(0, y)
    keep(1, slice(None), x)
    fill_weights()

    def to_owners(rows, parts, got, group, plane, n, at, axis):
        total, peak, mass = merged(parts)
        total = jnp.concatenate([total, peak_or_mass(peak, mass, n * NZ)], axis=1)
        for i in range(n * NZ):
            rows[i // NZ, i % NZ] = total[i : i + 1]
        for d, dz in plane:
            src = rows.at[lax.rem(at + d, n), lax.rem(z + dz, NZ)]
            remote(src, got.at[d * NZ + dz], group, **{axis: d}, dz=dz).start()
        got[0] = rows[at, z]

    one_wait(13, came_a, 18)
    one_wait(14, came_b, 19)
    one_wait(2, recv_a)
    parts = [noted(kept.at[0, y], notes_a.at[y])] + [noted(recv_a.at[d], came_a.at[d]) for d in range(NY - 1)]
    to_owners(rows_a, parts, got_a, 4, plane_a, NX, x, "dx")
    one_wait(3, recv_b)
    parts = [noted(kept.at[1, :, x], notes_b.at[x])] + [noted(recv_b.at[d], came_b.at[d]) for d in range(NX - 1)]
    to_owners(rows_b, parts, got_b, 5, plane_b, NY, y, "dy")
    fill_combine()

    one_wait(4, got_a.at[1:])
    one_wait(5, got_b.at[1:])
    k = y * 2 + c
    for p, got in enumerate((got_a, got_b)):
        total, peak, mass = unpacked(got[...].reshape(-1, WIDE))
        scale = jnp.exp(peak - jnp.max(peak, axis=0, keepdims=True))
        total, mass = (jnp.sum(a * scale, axis=0, keepdims=True) for a in (total, mass))
        inputs[k, :, HALF * p : HALF * (p + 1)] = total / mass

    for dy, dc in column:
        remote(inputs.at[k], inputs.at[k], 6, dy=dy, dc=dc).start()
    one_wait(6, inputs.at[1:])
    s_hi, s_lo = split(inputs[...].reshape(K, width))
    units = wih.shape[1]
    both = dot(jnp.concatenate([s_hi, s_lo], axis=0), wih[...])
    v = both[:K] + (both[K:] + dot(s_hi, wil[...]))
    slot = lax.broadcasted_iota(jnp.int32, v.shape, 0)
    unit = lax.broadcasted_iota(jnp.int32, v.shape, 1)
    own = slot // SLOTS == unit // (units // (K // SLOTS))
    hidden = jnp.where(own, v * (1.0 + lax.erf(v * 0.7071067811865476)) * 0.5, 0.0)
    h_hi, h_lo = split(hidden)
    both = dot(jnp.concatenate([h_hi, h_lo], axis=0), woh[...])
    partial = both[:K] + (both[K:] + dot(h_hi, wol[...]))
    for i in range(K):
        osend[i] = partial[i : i + 1]
    for i, (dy, dc) in enumerate(column):
        to = lax.rem(y + dy, NY) * 2 + lax.rem(c + dc, 2)
        remote(osend.at[to], orecv.at[i], 7, dy=dy, dc=dc).start()
    one_wait(7, orecv)
    total = osend[k]
    for i in range(len(column)):
        total += orecv[i]
    out_a[...] = total[:, :FIRST]
    out_b[...] = total[:, FIRST:]

    def to_plane(src, everything, group, plane, at, axis):
        row = at * NZ + z
        for d, dz in plane:
            remote(src, everything.at[row], group, **{axis: d}, dz=dz).start()
        everything[row] = src[...]

    to_plane(out_a, all_a, 8, plane_a, x, "dx")
    to_plane(out_b, all_b, 9, plane_b, y, "dy")

    def block(p, d, own=True):
        if p == 0:
            return (own_a if own else their_a).at[lax.rem(y + NY - d, NY)]
        return (own_b if own else their_b).at[:, lax.rem(x + NX - d, NX)]

    def pass_on(p, d):
        remote(block(p, d), block(p, d, False), 12 + 3 * p, 17 + 3 * p, dc=1).start()

    def spread(p, ds, axis):
        copies = {}
        for d in ds:
            copies[d] = remote(block(p, 0), block(p, 0), 10 + p, 10 + 3 * p + d, **{axis: d})
            copies[d].start()
        pass_on(p, 0)
        return copies

    one_wait(8, all_a.at[1:])
    own_a[y] = all_a[...].reshape(NX, NZ, FIRST)
    last_a = spread(0, ys, "dy")
    one_wait(9, all_b.at[1:])
    own_b[:, x] = all_b[...].reshape(NY, NZ, own_b.shape[-1])
    last_b = spread(1, xs, "dx")
    for d in reversed(ys):
        last_a[d].wait_recv()
        pass_on(0, d)
    for d in reversed(xs):
        last_b[d].wait_recv()
        pass_on(1, d)
    mixed[:, :FIRST] = dot3(oh[...], ol[...], *split(flat(own_a[...])))
    mixed[:, FIRST:] = dot3(oh[...], ol[...], *split(flat(own_b[...])))
    one_wait(12, their_a, 17)
    mixed[:, :FIRST] += dot3(ch[...], cl[...], *split(flat(their_a[...])))
    one_wait(15, their_b, 20)
    for copy in sends + whole:
        copy.wait_send()
    three_a, three_b = own_a.at[1:], own_b.at[:, 1:]
    remote(three_a, three_a, 10, dc=1).wait_send()
    remote(three_b, three_b, 11, dc=1).wait_send()


def mix_kernel(their_b, mixed, ch, cl, out_hbm, out, sem):
    ready = pl.ds(0, FIRST)
    copies = [pltpu.make_async_copy(mixed.at[:, ready], out_hbm.at[:, ready], sem.at[0])]
    copies[0].start()
    f_hi, f_lo = split(their_b[...].reshape(-1, their_b.shape[-1]))
    for i in range(0, out.shape[1], 256):
        at = pl.ds(FIRST + i, 256)
        part = dot3(ch[...], cl[...], f_hi[:, i : i + 256], f_lo[:, i : i + 256])
        out[:, i : i + 256] = mixed[:, FIRST + i : FIRST + i + 256] + part
        copies.append(pltpu.make_async_copy(out.at[:, pl.ds(i, 256)], out_hbm.at[:, at], sem.at[len(copies)]))
        copies[-1].start()
    for copy in copies:
        copy.wait()


def body(NX, NY, NZ, stop, tokens, slot_params, w_in, w_out):
    T, D = tokens.shape
    n_slots = slot_params.shape[1]
    E, H, _ = w_in.shape
    K = 2 * NY
    padded = -(-T // 128) * 128
    anywhere = pl.BlockSpec(memory_space=pltpu.MemorySpace.HBM)
    vmem = pltpu.VMEM
    dma = pltpu.SemaphoreType.DMA
    scratch = [
        vmem((T, D), F32), vmem((D, n_slots), F32), vmem((E, H, D), F32), vmem((E, H, D), F32),
        vmem((padded, D), BF16), vmem((padded, D), BF16),
        vmem((D, E * H), BF16), vmem((D, E * H), BF16), vmem((E * H, D), BF16), vmem((E * H, D), BF16),
        vmem((padded // 128, n_slots, 128), F32), vmem((n_slots, 128), F32),
        vmem((n_slots, padded), BF16), vmem((n_slots, padded), BF16),
        vmem((2, 2, NY, NX, NZ, WIDE), F32), vmem((2, NY, NX, NZ, WIDE), F32), vmem((2, NY, NX, NZ, HALF), F32), vmem((2, NY, NX, NZ, 128), F32),
        vmem((NY, NZ, 128), F32), vmem((NX, NZ, 128), F32), vmem((NY - 1, NZ, 128), F32), vmem((NX - 1, NZ, 128), F32),
        vmem((NY - 1, NX, NZ, HALF), F32), vmem((NX - 1, NY, NZ, HALF), F32),
        vmem((NX, NZ, 1, WIDE), F32), vmem((NY, NZ, 1, WIDE), F32),
        vmem((NX * NZ, 1, WIDE), F32), vmem((NY * NZ, 1, WIDE), F32),
        vmem((K, 1, D), F32), vmem((K, 1, D), F32), vmem((K - 1, 1, D), F32), vmem((1, FIRST), F32), vmem((1, D - FIRST), F32),
        vmem((NX * NZ, 1, FIRST), F32), vmem((NY * NZ, 1, D - FIRST), F32),
        vmem((NY, NX, NZ, FIRST), F32), vmem((NY, NX, NZ, D - FIRST), F32), vmem((NY, NX, NZ, FIRST), F32),
        vmem((T, n_slots // 2), BF16), vmem((T, n_slots // 2), BF16),
    ]
    scratch += [dma((2 * (D // 256) + 2,)), dma((16,)), dma((21,))]
    args = [pltpu.with_memory_space_constraint(a, pltpu.MemorySpace.HBM) for a in (tokens, slot_params, w_in, w_out)]
    results = pl.pallas_call(
        functools.partial(layer_kernel, NX, NY, NZ, stop),
        out_shape=(
            jax.ShapeDtypeStruct((NY, NX, NZ, D - FIRST), F32),
            jax.ShapeDtypeStruct((T, D), F32),
            jax.ShapeDtypeStruct((T, n_slots // 2), BF16),
            jax.ShapeDtypeStruct((T, n_slots // 2), BF16),
        ),
        in_specs=[anywhere] * 4,
        out_specs=(pl.BlockSpec(memory_space=pltpu.VMEM),) * 4,
        scratch_shapes=scratch,
        compiler_params=pltpu.CompilerParams(
            collective_id=0, has_side_effects=True, vmem_limit_bytes=40 * 1024 * 1024
        ),
        name="layer",
    )(*args)
    return pl.pallas_call(
        mix_kernel,
        out_shape=jax.ShapeDtypeStruct((T, D), F32),
        in_specs=[pl.BlockSpec(memory_space=pltpu.VMEM)] * 4,
        out_specs=anywhere,
        scratch_shapes=[vmem((T, D - FIRST), F32), dma((1 + (D - FIRST) // 256,))],
        compiler_params=pltpu.CompilerParams(vmem_limit_bytes=16 * 1024 * 1024),
        name="mix",
    )(*results)


def solution(mesh, NX=4, NY=4, NZ=8, stop=99):
    torus = Mesh(mesh.devices.reshape(NX, NZ, NY // 2, 2, mesh.shape["fsdp"]), AXES)
    every = ("x", "z", "y_lo", "core", "y_hi")
    return jax.shard_map(
        functools.partial(body, NX, NY, NZ, stop),
        mesh=torus,
        in_specs=(
            P(every, None),
            P(),
            P(("x", "z"), ("y_lo", "core", "y_hi"), None),
            P(("x", "z"), ("y_lo", "core", "y_hi"), None),
        ),
        out_specs=P(every, None),
        check_vma=False,
    )
```
